128 devices in a mesh: row: 4 (over z), col: 32 (over x, y, core).
Axes of the slice: x: 4, y: 4, z: 4, core: 2. Of those that a mesh axis runs over, the one named last changes fastest.
Arguments:
- fields: bfloat16 [8, 256, 32, 32, 128], P('row', 'col'), may hold values from -6 to 6
- wet_mask: int32 [8, 256], P('row', 'col'), may hold values from 0 to 1, as said below
- seam_flags: int32 [8, 256, 2], P('row', 'col'), may hold values from 0 to 1, as said below
- wet_list: int32 [1024], P(('row', 'col')), may hold values from 0 to 2047, as said below
- kernel_one: bfloat16 [3, 3, 128, 128], replicated, may hold values from -0.1875 to 0.1875
- bias_one: float32 [128], replicated, may hold values from -3 to 3
- kernel_two: bfloat16 [3, 3, 128, 128], replicated, may hold values from -0.1875 to 0.1875
- bias_two: float32 [128], replicated, may hold values from -3 to 3
- mixing: bfloat16 [128, 128], replicated, may hold values from -0.5 to 0.5
Outputs:
- updated: bfloat16 [1024, 32, 32, 128], P(('row', 'col'))
The draws below stay inside these ranges and needn't reach their ends.
Inputs may be any that keep to these rules, and one draw needn't show every extreme that they name: `wet_mask`: every group of 2 tile rows holds exactly 256 wet tiles, and in every such group some block of 2 x 8 tiles starting at a tile column k * 8 is all wet. `wet_list`: number the wet tiles of tile-row group r (tile rows r * 2 to r * 2 + 1) from 0: block by block along the tile columns (blocks of 2 x 8 tiles starting at tile columns k * 8), within a block row by row. Slot (r * 32 + c) * 8 + s holds the tile number (tile row times 256 plus tile column) of that group's wet tile c + 32 * s. `seam_flags`: nonzero only on the west side of tiles whose tile column is a positive multiple of 8 and on the east side of the tile to their west, both with the same value.
All inputs are finite; a program needn't handle non-finite values.
Results may differ from the reference program's by a relative error of at most 0.0039.
Values may be sent and summed in bfloat16 or wider, within the bound.
No kernel may reach another device: no remote copies, remote signals or barrier semaphores. Data moves between devices by JAX's collectives and lax.ppermute only.
A program may use at most 128 MiB of HBM per device.

```python
import jax
import jax.numpy as jnp
from jax import lax

C = 128
TILE = 32
TR_DEV = 2
TC_DEV = 8
WET_DEV = 8
TR = 8
TC = 256
N_ROW = 4
N_COL = 32


def wet_layout(key):
    face_dev = TR_DEV * TC_DEV
    halves = N_COL // 2
    even_counts = jax.random.randint(jax.random.fold_in(key, 11), (N_ROW, halves), 0, face_dev + 1)
    forced = jax.random.randint(jax.random.fold_in(key, 12), (N_ROW,), 0, halves)
    sides = jax.random.randint(jax.random.fold_in(key, 13), (N_ROW,), 0, 2)
    even_counts = jnp.where(jnp.arange(halves)[None, :] == forced[:, None], (sides * face_dev)[:, None], even_counts)
    counts = jnp.stack([even_counts, face_dev - even_counts], axis=2).reshape(N_ROW, N_COL)
    scores = jax.random.randint(jax.random.fold_in(key, 14), (N_ROW, N_COL, face_dev), 0, 1 << 20) * face_dev + jnp.arange(face_dev)
    ordering = jnp.argsort(scores, axis=2, stable=True)
    ranking = jnp.argsort(ordering, axis=2, stable=True)
    return (ranking < counts[:, :, None]).astype(jnp.int32)


def draw_wet_mask(key, part):
    layout = wet_layout(key).reshape(N_ROW, N_COL, TR_DEV, TC_DEV)
    return jnp.transpose(layout, (0, 2, 1, 3)).reshape(TR_DEV * N_ROW, TC_DEV * N_COL).astype(jnp.int32)


def draw_wet_list(key, part):
    face_dev = TR_DEV * TC_DEV
    layout = wet_layout(key).reshape(N_ROW, N_COL * face_dev)
    ranking = jnp.cumsum(layout, axis=1) - 1
    position = jnp.arange(N_COL * face_dev)[None, :]
    group_ids = jnp.arange(N_ROW)[:, None]
    block_col = position // face_dev
    inner_row = position % face_dev // TC_DEV
    inner_col = position % TC_DEV
    tile_number = (group_ids * TR_DEV + inner_row) * (TC_DEV * N_COL) + block_col * TC_DEV + inner_col
    slot_index = (group_ids * N_COL + ranking % N_COL) * WET_DEV + ranking // N_COL
    total_slots = N_ROW * N_COL * WET_DEV
    slot_index = jnp.where(layout == 1, slot_index, total_slots)
    listing = jnp.zeros((total_slots,), jnp.int32)
    listing = listing.at[slot_index.reshape(-1)].set(tile_number.reshape(-1).astype(jnp.int32), mode='drop')
    return listing


def draw_seam_flags(key, part):
    grid_rows = TR_DEV * N_ROW
    grid_cols = TC_DEV * N_COL
    boundary = jax.random.randint(jax.random.fold_in(key, 21), (grid_rows, N_COL), 0, 2)
    column_ids = jnp.arange(grid_cols)
    west_seam = jnp.where((column_ids % TC_DEV == 0) & (column_ids > 0), boundary[:, column_ids // TC_DEV], 0)
    east_pick = jnp.minimum((column_ids + 1) // TC_DEV, N_COL - 1)
    east_seam = jnp.where((column_ids % TC_DEV == TC_DEV - 1) & (column_ids + 1 < grid_cols), boundary[:, east_pick], 0)
    return jnp.stack([west_seam, east_seam], axis=2).astype(jnp.int32)


def level_of(stream_key, dims, split, least, top_value):
    loudness = 1.0
    for dim, parts in split:
        draws = jax.random.uniform(jax.random.fold_in(jax.random.fold_in(stream_key, 6), dim), (parts,), jnp.float32, least / len(split), top_value / len(split))
        loudness = loudness * jnp.repeat(jnp.exp(draws), dims[dim] // parts).reshape((-1,) + (1,) * (len(dims) - 1 - dim))
    return loudness


def normal_values(key, extent, spread, bound, pieces=(), held_as=jnp.bfloat16):
    factor_of = level_of(key, extent, pieces, -0.22, 0.18) if pieces else 1.0
    entries = jax.random.normal(key, extent, jnp.float32) * spread * factor_of
    return jnp.minimum(jnp.maximum(entries, -bound), bound).astype(held_as)


def setup_inputs(seed: int = 0) -> dict:
    arg_keys = jax.random.split(jax.random.key(seed), 10)
    fields = normal_values(arg_keys[0], (TR, TC, TILE, TILE, C), 1.0, 6.0, ((0, 4), (1, 32)))
    wet_mask = draw_wet_mask(jax.random.fold_in(arg_keys[9], 71), 0)
    seam_flags = draw_seam_flags(jax.random.fold_in(arg_keys[9], 71), 0)
    wet_list = draw_wet_list(jax.random.fold_in(arg_keys[9], 71), 0)
    kernel_one = normal_values(arg_keys[4], (3, 3, C, C), (9 * C) ** -0.5, 0.1875)
    bias_one = normal_values(arg_keys[5], (C,), 0.5, 3.0, (), jnp.float32)
    kernel_two = normal_values(arg_keys[6], (3, 3, C, C), (9 * C) ** -0.5, 0.1875)
    bias_two = normal_values(arg_keys[7], (C,), 0.5, 3.0, (), jnp.float32)
    mixing = normal_values(arg_keys[8], (C, C), C ** -0.5, 0.5)
    return {"fields": fields, "wet_mask": wet_mask, "seam_flags": seam_flags, "wet_list": wet_list, "kernel_one": kernel_one, "bias_one": bias_one, "kernel_two": kernel_two, "bias_two": bias_two, "mixing": mixing}


def window_tiles(padded, tile_side, seam_part):
    rows_all = padded.shape[0] - 2
    cols_all = padded.shape[1] - 2
    row_tiles = rows_all // tile_side
    col_tiles = cols_all // tile_side
    channels = padded.shape[2]
    core_rows = padded[1:rows_all + 1].reshape(row_tiles, tile_side, cols_all + 2, channels)
    above = padded[0:rows_all:tile_side][:, None]
    below = padded[tile_side + 1::tile_side][:, None]
    stacked = jnp.concatenate([above, core_rows, below], axis=1)
    inner = stacked[:, :, 1:cols_all + 1].reshape(row_tiles, tile_side + 2, col_tiles, tile_side, channels)
    west_cols = stacked[:, :, 0:cols_all:tile_side][:, :, :, None]
    east_cols = stacked[:, :, tile_side + 1::tile_side][:, :, :, None]
    tile_set = jnp.concatenate([west_cols, inner, east_cols], axis=3)
    tile_set = jnp.transpose(tile_set, (0, 2, 1, 3, 4))
    west_edge = tile_set[:, :, 1:tile_side + 1, 0]
    east_edge = tile_set[:, :, 1:tile_side + 1, tile_side + 1]
    west_edge = jnp.where(seam_part[:, :, 0, None, None] == 1, west_edge[:, :, ::-1], west_edge)
    east_edge = jnp.where(seam_part[:, :, 1, None, None] == 1, east_edge[:, :, ::-1], east_edge)
    tile_set = tile_set.at[:, :, 1:tile_side + 1, 0].set(west_edge)
    tile_set = tile_set.at[:, :, 1:tile_side + 1, tile_side + 1].set(east_edge)
    return tile_set


def convolve(tile_set, kernel, bias_row):
    count_all = tile_set.shape[0]
    tile_side = tile_set.shape[1] - 2
    channels = tile_set.shape[3]
    values = tile_set.astype(jnp.float32)
    weights = kernel.astype(jnp.float32)
    total = jnp.zeros((count_all * tile_side * tile_side, kernel.shape[3]), jnp.float32)
    for shift_row in range(3):
        for shift_col in range(3):
            window = values[:, shift_row:shift_row + tile_side, shift_col:shift_col + tile_side].reshape(-1, channels)
            total = total + jnp.dot(window, weights[shift_row, shift_col], preferred_element_type=jnp.float32, precision=lax.Precision.HIGHEST)
    return (total + bias_row).reshape(count_all, tile_side, tile_side, -1)


def layer_grid(activation, seam_flags, kernel, bias_row):
    grid_rows, grid_cols, tile_side = activation.shape[0], activation.shape[1], activation.shape[2]
    channels = activation.shape[4]
    pixels = jnp.transpose(activation, (0, 2, 1, 3, 4)).reshape(grid_rows * tile_side, grid_cols * tile_side, channels)
    padded = jnp.pad(pixels, ((1, 1), (1, 1), (0, 0)))

    def one_row(row_index):
        slab = lax.dynamic_slice_in_dim(padded, row_index * tile_side, tile_side + 2, 0)
        flags = lax.dynamic_slice_in_dim(seam_flags, row_index, 1, 0)
        tile_set = window_tiles(slab, tile_side, flags)[0]
        result = convolve(tile_set, kernel, bias_row)
        return jax.nn.gelu(result).astype(jnp.bfloat16)

    return lax.map(one_row, jnp.arange(grid_rows, dtype=jnp.int32))


def reference(fields, wet_mask, seam_flags, wet_list, kernel_one, bias_one, kernel_two, bias_two, mixing):
    grid_cols = fields.shape[1]
    channels = fields.shape[4]
    wet_scale = wet_mask.astype(fields.dtype)[:, :, None, None, None]
    masked = fields * wet_scale
    hidden = layer_grid(masked, seam_flags, kernel_one, bias_one) * wet_scale
    second = layer_grid(hidden, seam_flags, kernel_two, bias_two)
    tile_rows = (wet_list // grid_cols).astype(jnp.int32)
    tile_cols = (wet_list % grid_cols).astype(jnp.int32)
    residual = masked[tile_rows, tile_cols]
    branch = second[tile_rows, tile_cols].astype(jnp.float32)
    mixed = jnp.dot(branch.reshape(-1, channels), mixing.astype(jnp.float32), preferred_element_type=jnp.float32, precision=lax.Precision.HIGHEST)
    return (residual.astype(jnp.float32) + mixed.reshape(residual.shape)).astype(jnp.bfloat16)
```

```python
import functools

import jax
import jax.numpy as jnp
from jax import lax
from jax.experimental import pallas as pl
from jax.experimental.pallas import tpu as pltpu
from jax.sharding import PartitionSpec as P

F32 = jnp.float32
BF16 = jnp.bfloat16
VMEM_LIMIT = 56 * 1024 * 1024
WHOLE = pl.BlockSpec(memory_space=pltpu.VMEM)
SCALARS = pl.BlockSpec(memory_space=pltpu.SMEM)
IN_PLACE = pl.BlockSpec(memory_space=pl.ANY)


def dot(a, b):
    return jnp.dot(a, b, preferred_element_type=F32)


def gelu(x):
    u = x * (0.7978845608028654 + 0.03567740813636141 * (x * x))
    half = 0.5 * x
    return half + half * jnp.tanh(u)


def fill_weights(k_ref, w_ref):
    ch = k_ref.shape[2]
    zero = jnp.zeros((ch, 3 * ch), BF16)
    w_ref[3 * ch :, : 3 * ch] = zero
    w_ref[:ch, 3 * ch :] = zero
    for dy in range(3):
        for dx in range(3):
            block = k_ref[dy, dx]
            w_ref[dy * ch : (dy + 1) * ch, dx * ch : (dx + 1) * ch] = block
            w_ref[(dy + 1) * ch : (dy + 2) * ch, (3 + dx) * ch : (4 + dx) * ch] = block


def fill_edges(ext_ref, flag_ref, side, k_ref, dx, pad_ref, z_ref, tr_dev, tile):
    ext = ext_ref[...].astype(F32)
    rows = lax.broadcasted_iota(jnp.int32, (tile, tile), 0)
    cols = lax.broadcasted_iota(jnp.int32, (tile, tile), 1)
    flip = jnp.where(rows + cols == tile - 1, 1.0, 0.0).astype(BF16)
    for i in range(tr_dev):
        part = ext[i * tile : i * tile + tile + 2]
        pad_ref[0 : tile + 2] = part
        middle = pad_ref[1 : tile + 1]
        turned = dot(flip, middle.astype(BF16))
        pad_ref[1 : tile + 1] = jnp.where(flag_ref[2 * i + side] == 1, turned, middle)
        total = dot(pad_ref[0:tile].astype(BF16), k_ref[0, dx])
        total += dot(pad_ref[1 : tile + 1].astype(BF16), k_ref[1, dx])
        total += dot(pad_ref[2 : tile + 2].astype(BF16), k_ref[2, dx])
        z_ref[i * tile : (i + 1) * tile] = total


def conv_pair(window, w_ref, bias, zw_ref, ze_ref, row):
    ch = window[0].shape[1]
    width = window[0].shape[0]
    z = dot(jnp.concatenate(window, axis=1), w_ref[...])
    lane_row = lax.broadcasted_iota(jnp.int32, (8, ch), 0)
    outs = []
    for ro in range(2):
        base = 3 * ro * ch
        left = pltpu.roll(z[:, base : base + ch], 1, 0)
        right = pltpu.roll(z[:, base + 2 * ch : base + 3 * ch], width - 1, 0)
        west = zw_ref[pl.ds(row + ro, 1), :]
        east = ze_ref[pl.ds(row + ro, 1), :]
        left = jnp.concatenate([jnp.where(lane_row == 0, west, left[:8]), left[8:]], axis=0)
        right = jnp.concatenate(
            [right[: width - 8], jnp.where(lane_row == 7, east, right[width - 8 :])], axis=0
        )
        outs.append(z[:, base + ch : base + 2 * ch] + left + right + bias)
    return outs


def span_of(height):
    return height // 4


def first_kernel(
    wet_ref, flag_ref, fields_ref, north_ref, south_ref, west_ref, east_ref, k_ref, b_ref,
    hid_out, lcol_ref, rcol_ref,
    f_ref, x_ref, hid_ref, w_ref, pad_ref, zw_ref, ze_ref, m_ref, lc_ref, rc_ref, in_sems, out_sems,
):
    tr_dev, tc_dev, tile, _, ch = fields_ref.shape
    width = tc_dev * tile
    height = tr_dev * tile
    span = span_of(height)
    loads = [
        pltpu.make_async_copy(fields_ref.at[i], f_ref.at[i], in_sems.at[i]) for i in range(tr_dev)
    ]
    for load in loads:
        load.start()
    fill_weights(k_ref, w_ref)
    fill_edges(west_ref, flag_ref, 0, k_ref, 0, pad_ref, zw_ref, tr_dev, tile)
    fill_edges(east_ref, flag_ref, 1, k_ref, 2, pad_ref, ze_ref, tr_dev, tile)
    x_ref[0] = north_ref[...]
    x_ref[height + 1] = south_ref[...]
    bias = b_ref[...]

    def fill(i):
        loads[i].wait()
        for j in range(tc_dev):
            wet = wet_ref[i * tc_dev + j].astype(F32)
            scale = jnp.full((1, ch), 1.0, F32) * wet
            m_ref[i, j * tile : (j + 1) * tile] = jnp.broadcast_to(scale, (tile, ch))
            x_ref[1 + i * tile : 1 + (i + 1) * tile, j * tile : (j + 1) * tile] = (
                f_ref[i, j] * scale.astype(BF16)[None]
            )

    def step(p, carry):
        row = 2 * p
        window = [x_ref[row + k] for k in range(4)]
        outs = conv_pair(window, w_ref, bias, zw_ref, ze_ref, row)
        for ro in range(2):
            value = gelu(outs[ro]) * m_ref[p // (tile // 2)]
            hid_ref[row + ro] = value.astype(BF16)
            lc_ref[pl.ds(row + ro, 1), :] = value[0:1]
            rc_ref[pl.ds(row + ro, 1), :] = value[width - 1 : width]
        return carry

    stores = [
        pltpu.make_async_copy(
            hid_ref.at[pl.ds(g * span, span)], hid_out.at[pl.ds(g * span, span)], out_sems.at[g]
        )
        for g in range(4)
    ]
    filled = 0
    for g in range(4):
        while filled < tr_dev and (g + 1) * span >= filled * tile:
            fill(filled)
            filled += 1
        lax.fori_loop(g * span // 2, (g + 1) * span // 2, step, 0, unroll=4)
        stores[g].start()
    lcol_ref[...] = lc_ref[...].astype(BF16)
    rcol_ref[...] = rc_ref[...].astype(BF16)
    for store in stores:
        store.wait()


def second_kernel(
    dst_ref, flag_ref, hid_hbm, fields_ref, north_ref, south_ref, west_ref, east_ref, k_ref, b_ref,
    mix_ref, keep_ref, give_ref,
    hid_ref, out_ref, w_ref, pad_ref, zw_ref, ze_ref, mm_ref, hid_sems, in_sems, sems,
):
    tr_dev, tc_dev, tile, _, ch = fields_ref.shape
    width = tc_dev * tile
    height = tr_dev * tile
    span = span_of(height)
    slots = keep_ref.shape[0]
    hid_loads = [
        pltpu.make_async_copy(
            hid_hbm.at[pl.ds(g * span, span)], hid_ref.at[pl.ds(1 + g * span, span)], hid_sems.at[g]
        )
        for g in range(4)
    ]
    loads = [
        pltpu.make_async_copy(fields_ref.at[i], out_ref.at[i], in_sems.at[i]) for i in range(tr_dev)
    ]
    hid_loads[0].start()
    hid_loads[1].start()
    loads[0].start()
    hid_loads[2].start()
    hid_loads[3].start()
    for load in loads[1:]:
        load.start()
    fill_weights(k_ref, w_ref)
    fill_edges(west_ref, flag_ref, 0, k_ref, 0, pad_ref, zw_ref, tr_dev, tile)
    fill_edges(east_ref, flag_ref, 1, k_ref, 2, pad_ref, ze_ref, tr_dev, tile)
    zero = jnp.zeros((ch, ch), BF16)
    mm_ref[:ch, :ch] = mix_ref[...]
    mm_ref[ch:, ch:] = mix_ref[...]
    mm_ref[:ch, ch:] = zero
    mm_ref[ch:, :ch] = zero
    hid_ref[0] = north_ref[...]
    hid_ref[height + 1] = south_ref[...]
    bias = b_ref[...]

    def copies(i, act):
        for j in range(tc_dev):
            k = i * tc_dev + j
            target = dst_ref[k]

            @pl.when((target >= 0) & (target < slots))
            def _():
                act(pltpu.make_async_copy(out_ref.at[i, j], keep_ref.at[target], sems.at[k]))

            @pl.when(target >= slots)
            def _():
                act(pltpu.make_async_copy(out_ref.at[i, j], give_ref.at[target - slots], sems.at[k]))

    def step(p, carry):
        row = 2 * p
        i = row // tile
        inner = row % tile
        window = [hid_ref[row + k] for k in range(4)]
        outs = conv_pair(window, w_ref, bias, zw_ref, ze_ref, row)
        branch = jnp.concatenate([gelu(o).astype(BF16) for o in outs], axis=1)
        mixed = dot(branch, mm_ref[...])
        for ro in range(2):
            own = out_ref[i, :, inner + ro].reshape(width, ch).astype(F32)
            total = (own + mixed[:, ro * ch : (ro + 1) * ch]).astype(BF16)
            out_ref[i, :, inner + ro] = total.reshape(tc_dev, tile, ch)
        return carry

    hid_loads[0].wait()
    for g in range(4):
        if g < 3:
            hid_loads[g + 1].wait()
        if g * span % tile == 0:
            loads[g * span // tile].wait()
        lax.fori_loop(g * span // 2, (g + 1) * span // 2, step, 0, unroll=4)
        if (g + 1) * span % tile == 0:
            copies(g * span // tile, lambda c: c.start())
    for i in range(tr_dev):
        copies(i, lambda c: c.wait())


def scatter_kernel(dst_ref, src_ref, held_ref, out_ref, buf_ref, in_sems, sems):
    def each(act):
        for k in range(src_ref.shape[0]):

            @pl.when(dst_ref[k] >= 0)
            def _():
                act(k)

    def load(k):
        return pltpu.make_async_copy(src_ref.at[k], buf_ref.at[k], in_sems.at[k])

    def store(k):
        return pltpu.make_async_copy(buf_ref.at[k], out_ref.at[dst_ref[k]], sems.at[k])

    def turn(k):
        load(k).wait()
        store(k).start()

    each(lambda k: load(k).start())
    each(turn)
    each(lambda k: store(k).wait())


def gather_kernel(idx_ref, src_ref, out_ref, buf_ref, in_sems, sems):
    count = out_ref.shape[0]

    def load(k):
        return pltpu.make_async_copy(src_ref.at[idx_ref[k]], buf_ref.at[k], in_sems.at[k])

    def store(k):
        return pltpu.make_async_copy(buf_ref.at[k], out_ref.at[k], sems.at[k])

    for k in range(count):
        load(k).start()
    for k in range(count):
        load(k).wait()
        store(k).start()
    for k in range(count):
        store(k).wait()


def shifted(x, axis, step):
    count = lax.axis_size(axis)
    pairs = [(i, i + step) for i in range(count) if 0 <= i + step < count]
    return lax.ppermute(x, axis, pairs)


def halos(top, bottom, left, right):
    north = shifted(bottom, "row", 1)
    south = shifted(top, "row", -1)
    left = jnp.concatenate([north[:1], left, south[:1]], axis=0)
    right = jnp.concatenate([north[-1:], right, south[-1:]], axis=0)
    return north, south, shifted(right, "col", 1), shifted(left, "col", -1)


def on_device(
    fields, wet_mask, seam_flags, wet_list, kernel_one, bias_one, kernel_two, bias_two, mixing
):
    tr_dev, tc_dev, tile, _, ch = fields.shape
    face = tr_dev * tc_dev
    wet_dev = wet_list.shape[0]
    columns = lax.axis_size("col")
    chips = columns // 2
    width, height = tc_dev * tile, tr_dev * tile
    me = lax.axis_index("col")
    core = me % 2
    wet = wet_mask.reshape(face)
    flags = jnp.stack([seam_flags[:, 0, 0], seam_flags[:, tc_dev - 1, 1]], axis=1).reshape(-1)

    total = jnp.broadcast_to(jnp.sum(wet), (columns, 1, 1))
    counts = lax.all_to_all(total, "col", split_axis=0, concat_axis=0, tiled=True).reshape(columns)
    cids = jnp.arange(columns)
    start = jnp.sum(jnp.where(cids < me, counts, 0))
    mate = me ^ 1
    mate_start = jnp.sum(jnp.where(cids < mate, counts, 0))
    mate_count = jnp.sum(jnp.where(cids == mate, counts, 0))
    ids = jnp.arange(face)
    local = jnp.sum(jnp.where(ids[None, :] < ids[:, None], wet[None, :], 0), axis=1)
    rank = start + local
    slot = (rank % columns) // 2
    dst = jnp.where(wet == 1, jnp.where(rank % 2 == core, slot, chips + local // 2), -1)
    half = face // 2
    mate_local = 2 * jnp.arange(half) + (mate_start + core) % 2
    mate_dst = jnp.where(mate_local < mate_count, ((mate_start + mate_local) % columns) // 2, -1)
    source_chip = (wet_list % (tc_dev * columns)) // (2 * tc_dev)

    scale = wet_mask.astype(BF16)
    top = (fields[0, :, 0] * scale[0, :, None, None]).reshape(width, ch)
    bottom = (fields[-1, :, -1] * scale[-1, :, None, None]).reshape(width, ch)
    left = (fields[:, 0, :, 0] * scale[:, 0, None, None]).reshape(height, ch)
    right = (fields[:, -1, :, -1] * scale[:, -1, None, None]).reshape(height, ch)
    params = pltpu.CompilerParams(vmem_limit_bytes=VMEM_LIMIT)
    hid, lcol, rcol = pl.pallas_call(
        first_kernel,
        out_shape=(
            jax.ShapeDtypeStruct((height, width, ch), BF16),
            jax.ShapeDtypeStruct((height, ch), BF16),
            jax.ShapeDtypeStruct((height, ch), BF16),
        ),
        in_specs=[SCALARS, SCALARS, IN_PLACE] + [WHOLE] * 6,
        out_specs=(IN_PLACE, WHOLE, WHOLE),
        scratch_shapes=[
            pltpu.VMEM(fields.shape, BF16),
            pltpu.VMEM((height + 2, width, ch), BF16),
            pltpu.VMEM((height, width, ch), BF16),
            pltpu.VMEM((4 * ch, 6 * ch), BF16),
            pltpu.VMEM((tile + 8, ch), F32),
            pltpu.VMEM((height, ch), F32),
            pltpu.VMEM((height, ch), F32),
            pltpu.VMEM((tr_dev, width, ch), F32),
            pltpu.VMEM((height, ch), F32),
            pltpu.VMEM((height, ch), F32),
            pltpu.SemaphoreType.DMA((tr_dev,)),
            pltpu.SemaphoreType.DMA((4,)),
        ],
        compiler_params=params,
        name="first_conv",
    )(wet, flags, fields, *halos(top, bottom, left, right), kernel_one, bias_one[None])

    tile_shape = (tile, tile, ch)
    keep, give = pl.pallas_call(
        second_kernel,
        out_shape=(
            jax.ShapeDtypeStruct((chips,) + tile_shape, BF16),
            jax.ShapeDtypeStruct((half,) + tile_shape, BF16),
        ),
        in_specs=[SCALARS, SCALARS, IN_PLACE, IN_PLACE] + [WHOLE] * 7,
        out_specs=(IN_PLACE, IN_PLACE),
        scratch_shapes=[
            pltpu.VMEM((height + 2, width, ch), BF16),
            pltpu.VMEM((tr_dev, tc_dev) + tile_shape, BF16),
            pltpu.VMEM((4 * ch, 6 * ch), BF16),
            pltpu.VMEM((tile + 8, ch), F32),
            pltpu.VMEM((height, ch), F32),
            pltpu.VMEM((height, ch), F32),
            pltpu.VMEM((2 * ch, 2 * ch), BF16),
            pltpu.SemaphoreType.DMA((4,)),
            pltpu.SemaphoreType.DMA((tr_dev,)),
            pltpu.SemaphoreType.DMA((face,)),
        ],
        compiler_params=params,
        name="second_conv",
    )(
        dst, flags, hid, fields, *halos(hid[0], hid[-1], lcol, rcol),
        kernel_two, bias_two[None], mixing,
    )

    taken = lax.ppermute(give, "col", [(i, i ^ 1) for i in range(columns)])
    sending = pl.pallas_call(
        scatter_kernel,
        out_shape=jax.ShapeDtypeStruct(keep.shape, BF16),
        in_specs=[SCALARS, IN_PLACE, IN_PLACE],
        out_specs=IN_PLACE,
        scratch_shapes=[
            pltpu.VMEM((half,) + tile_shape, BF16),
            pltpu.SemaphoreType.DMA((half,)),
            pltpu.SemaphoreType.DMA((half,)),
        ],
        input_output_aliases={2: 0},
        name="merge_mate",
    )(mate_dst, taken, keep)
    groups = [[2 * k + c for k in range(chips)] for c in range(2)]
    arrived = lax.all_to_all(
        sending, "col", split_axis=0, concat_axis=0, tiled=True, axis_index_groups=groups
    )
    return pl.pallas_call(
        gather_kernel,
        out_shape=jax.ShapeDtypeStruct((wet_dev,) + tile_shape, BF16),
        in_specs=[SCALARS, IN_PLACE],
        out_specs=IN_PLACE,
        scratch_shapes=[
            pltpu.VMEM((wet_dev,) + tile_shape, BF16),
            pltpu.SemaphoreType.DMA((wet_dev,)),
            pltpu.SemaphoreType.DMA((wet_dev,)),
        ],
        name="slot_order",
    )(source_chip, arrived)


def solution(mesh):
    return jax.shard_map(
        on_device,
        mesh=mesh,
        in_specs=(
            P("row", "col", None, None, None),
            P("row", "col"),
            P("row", "col", None),
            P(("row", "col")),
            P(),
            P(),
            P(),
            P(),
            P(),
        ),
        out_specs=P(("row", "col"), None, None, None),
        check_vma=False,
    )
```

```python
import functools

import jax
import jax.numpy as jnp
from jax import lax
from jax.experimental import pallas as pl
from jax.experimental.pallas import tpu as pltpu
from jax.sharding import PartitionSpec as P

F32 = jnp.float32
BF16 = jnp.bfloat16
VMEM_LIMIT = 56 * 1024 * 1024
WHOLE = pl.BlockSpec(memory_space=pltpu.VMEM)
SCALARS = pl.BlockSpec(memory_space=pltpu.SMEM)
IN_PLACE = pl.BlockSpec(memory_space=pl.ANY)


def dot(a, b):
    return jnp.dot(a, b, preferred_element_type=F32)


def gelu(x):
    u = x * (0.7978845608028654 + 0.03567740813636141 * (x * x))
    half = 0.5 * x
    return half + half * jnp.tanh(u)


def fill_weights(k_ref, w_ref):
    ch = k_ref.shape[2]
    zero = jnp.zeros((ch, 3 * ch), BF16)
    w_ref[3 * ch :, : 3 * ch] = zero
    w_ref[:ch, 3 * ch :] = zero
    for dy in range(3):
        for dx in range(3):
            block = k_ref[dy, dx]
            w_ref[dy * ch : (dy + 1) * ch, dx * ch : (dx + 1) * ch] = block
            w_ref[(dy + 1) * ch : (dy + 2) * ch, (3 + dx) * ch : (4 + dx) * ch] = block


def tall_conv(t_ref, k_ref, dx, count):
    total = dot(t_ref[0:count].astype(BF16), k_ref[0, dx])
    total += dot(t_ref[1 : count + 1].astype(BF16), k_ref[1, dx])
    total += dot(t_ref[2 : count + 2].astype(BF16), k_ref[2, dx])
    return total


def put_columns(t_ref, col_ref, base, tr_dev, tile):
    tall = tile + 2
    t_ref[0:3] = col_ref[base : base + 3]
    for i in range(tr_dev):
        t_ref[3 + tall * i : 3 + tall * (i + 1)] = col_ref[
            base + 1 + tile * i : base + 1 + tile * i + tall
        ]
    last = 3 + tall * tr_dev
    t_ref[last : last + 3] = col_ref[base + 1 + tile * tr_dev : base + 4 + tile * tr_dev]


def put_pads(t_ref, above, ext_ref, base, flags, below, flip, tile):
    tall = tile + 2
    for n, line in enumerate(above):
        t_ref[n : n + 1] = line
    for i, flag in enumerate(flags):
        at = 3 + tall * i
        from_row = base + tile * i
        t_ref[at : at + 1] = ext_ref[from_row : from_row + 1]
        middle = ext_ref[from_row + 1 : from_row + 1 + tile]
        turned = dot(flip, middle.astype(BF16))
        t_ref[at + 1 : at + 1 + tile] = jnp.where(flag == 1, turned, middle)
        t_ref[at + tall - 1 : at + tall] = ext_ref[from_row + tile + 1 : from_row + tile + 2]
    last = 3 + tall * len(flags)
    for n, line in enumerate(below):
        t_ref[last + n : last + n + 1] = line


def line_at(tall_row, tile):
    return 3 + tall_row + 2 * (tall_row // tile)


def side_sums(z, taps, west, east):
    ch = west.shape[1]
    width = z.shape[0]
    lane_row = lax.broadcasted_iota(jnp.int32, (8, ch), 0)
    left = pltpu.roll(z[:, taps : taps + ch], 1, 0)
    right = pltpu.roll(z[:, taps + 2 * ch : taps + 3 * ch], width - 1, 0)
    left = jnp.concatenate([jnp.where(lane_row == 0, west, left[:8]), left[8:]], axis=0)
    right = jnp.concatenate(
        [right[: width - 8], jnp.where(lane_row == 7, east, right[width - 8 :])], axis=0
    )
    return z[:, taps + ch : taps + 2 * ch] + left + right


def conv_pair(window, w_ref, bias, zw_ref, ze_ref, line):
    ch = window[0].shape[1]
    z = dot(jnp.concatenate(window, axis=1), w_ref[...])
    outs = []
    for ro in range(2):
        west = zw_ref[pl.ds(line + ro, 1), :]
        east = ze_ref[pl.ds(line + ro, 1), :]
        outs.append(side_sums(z, 3 * ro * ch, west, east) + bias)
    return outs


def rim_kernel(
    wet_ref, flag_ref, fields_ref, top_ref, bottom_ref, lcol_ref, rcol_ref,
    rows_ref, cols_ref, line_ref, sems,
):
    tr_dev, tc_dev, tile, _, ch = fields_ref.shape
    width, height = tc_dev * tile, tr_dev * tile
    part = cols_ref.shape[3]
    loads = [
        pltpu.make_async_copy(fields_ref.at[0, :, 0:2], rows_ref.at[0], sems.at[0]),
        pltpu.make_async_copy(fields_ref.at[tr_dev - 1, :, tile - 2 : tile], rows_ref.at[1], sems.at[1]),
        pltpu.make_async_copy(fields_ref.at[:, 0, :, 0:part], cols_ref.at[0], sems.at[2]),
        pltpu.make_async_copy(fields_ref.at[:, tc_dev - 1, :, tile - part :], cols_ref.at[1], sems.at[3]),
    ]
    for load in loads:
        load.start()
    for load in loads:
        load.wait()

    def wet(i, j):
        return jnp.full((1, ch), 1.0, F32) * wet_ref[i * tc_dev + j].astype(F32)

    for side, (out_ref, i) in enumerate(((top_ref, 0), (bottom_ref, tr_dev - 1))):
        for j in range(tc_dev):
            scale = wet(i, j).astype(BF16)
            for n in range(2):
                out_ref[n * width + j * tile : n * width + (j + 1) * tile] = (
                    rows_ref[side, j, n] * scale
                )
    picked = []
    for side, out_ref in enumerate((lcol_ref, rcol_ref)):
        for i in range(tr_dev):
            block = cols_ref[side, i].astype(F32) * wet(i, side * (tc_dev - 1))[None]
            line_ref[side, i * tile * part : (i + 1) * tile * part] = block.reshape(tile * part, ch)
        first = side * (part - 2)
        columns = [line_ref[side, pl.ds(first + n, height, stride=part)] for n in range(2)]
        out_ref[0] = columns[0].astype(BF16)
        out_ref[1] = columns[1].astype(BF16)
        picked.append(columns[side])
    for out_ref, i, near in ((top_ref, 0, tile - 2), (bottom_ref, tr_dev - 1, tile * (tr_dev - 1))):
        flags = [jnp.full((1, ch), 1.0, F32) * flag_ref[2 * i + side].astype(F32) for side in range(2)]
        extra = [column[near : near + 2] for column in picked]
        extra += [wet(i, j) for j in range(tc_dev)] + flags
        extra.append(jnp.zeros((12 - tc_dev - 2, ch), F32))
        at = 0
        for piece in extra:
            line_ref[0, at : at + piece.shape[0]] = piece
            at += piece.shape[0]
        out_ref[2 * width : 2 * width + 16] = line_ref[0, 0:16].astype(BF16)


def conv_kernel(
    wet_ref, flag_ref, dst_ref, fields_ref, north_ref, south_ref, west_ref, east_ref,
    lcol_ref, rcol_ref, k1_ref, b1_ref, k2_ref, b2_ref, mix_ref, keep_ref, give_ref,
    out_ref, x_ref, hid_ref, w1_ref, w2_ref, mm_ref, m_ref, pack_ref, own_ref, ext_ref, t_ref,
    zw1_ref, ze1_ref, zw2_ref, ze2_ref, in_sems, sems,
):
    tr_dev, tc_dev, tile, _, ch = fields_ref.shape
    width, height = tc_dev * tile, tr_dev * tile
    slots = keep_ref.shape[0]
    tall = 3 + (tile + 2) * tr_dev + 3
    lines = tall - 2
    loads = [
        pltpu.make_async_copy(fields_ref.at[i], out_ref.at[i], in_sems.at[i]) for i in range(tr_dev)
    ]
    for load in loads:
        load.start()
    fill_weights(k1_ref, w1_ref)
    fill_weights(k2_ref, w2_ref)
    zero = jnp.zeros((ch, ch), BF16)
    mm_ref[:ch, :ch] = mix_ref[...]
    mm_ref[ch:, ch:] = mix_ref[...]
    mm_ref[:ch, ch:] = zero
    mm_ref[ch:, :ch] = zero
    bias1 = b1_ref[...]
    bias2 = b2_ref[...]
    rows = lax.broadcasted_iota(jnp.int32, (tile, tile), 0)
    cols = lax.broadcasted_iota(jnp.int32, (tile, tile), 1)
    flip = jnp.where(rows + cols == tile - 1, 1.0, 0.0).astype(BF16)

    notes = [ref[2 * width : 2 * width + 16].astype(F32) for ref in (north_ref, south_ref)]
    flagged = [[note[4 + tc_dev + s : 5 + tc_dev + s] > 0.5 for s in range(2)] for note in notes]

    def pixel(ref, n):
        base = n // 16 * 16
        return ref[base : base + 16].astype(F32)[n - base : n - base + 1]

    step_size = pack_ref.shape[1] // 20 * 9
    sides = ((west_ref, lcol_ref, 0), (east_ref, rcol_ref, width - 1))
    for s, (pack, own, c) in enumerate(sides):
        pack_ref[s] = pack[...].astype(F32)
        own_ref[s, 1 : height + 1] = own[...].astype(F32)
        own_ref[s, 0:1] = pixel(north_ref, width + c)
        own_ref[s, height + 1 : height + 2] = pixel(south_ref, c)
    for s, (pack, own, c) in enumerate(sides):
        near = step_size * (1 - s)
        far = step_size * s
        notes_at = 2 * step_size
        note = [pack_ref[s, notes_at + n : notes_at + n + 1] for n in range(8)]
        held = pack_ref.at[s]
        mine = own_ref.at[s]
        flags = [flag_ref[2 * i + s] for i in range(tr_dev)]
        north_flag, south_flag = flagged[0][s], flagged[1][s]

        def near_line(n, near=near, held=held):
            return held[near + n : near + n + 1]

        above = [
            jnp.where(north_flag, note[1], near_line(0)),
            jnp.where(north_flag, note[0], near_line(1)),
            near_line(2),
        ]
        below = [
            near_line(height + 1),
            jnp.where(south_flag, note[3], near_line(height + 2)),
            jnp.where(south_flag, note[2], near_line(height + 3)),
        ]
        put_pads(t_ref.at[0], above, held, near + 1, flags, below, flip, tile)
        z_ref = (zw1_ref, ze1_ref)[s]
        z_ref[0:lines] = tall_conv(t_ref.at[0], k1_ref, 2 * s, lines)
        total = bias1
        put_columns(t_ref.at[1], held, near, tr_dev, tile)
        total = total + tall_conv(t_ref.at[1], k1_ref, 1, lines)
        put_columns(t_ref.at[2], held, far, tr_dev, tile)
        total = total + tall_conv(t_ref.at[2], k1_ref, 2 * s, lines)
        above = [
            jnp.where(north_flag, notes[0][2 * s + 1 : 2 * s + 2], pixel(north_ref, c)),
            jnp.where(north_flag, notes[0][2 * s : 2 * s + 1], pixel(north_ref, width + c)),
            mine[1:2],
        ]
        below = [
            mine[height : height + 1],
            jnp.where(south_flag, notes[1][2 * s + 1 : 2 * s + 2], pixel(south_ref, c)),
            jnp.where(south_flag, notes[1][2 * s : 2 * s + 1], pixel(south_ref, width + c)),
        ]
        put_pads(t_ref.at[3], above, mine, 0, flags, below, flip, tile)
        total = total + tall_conv(t_ref.at[3], k1_ref, 2 - 2 * s, lines)
        value = gelu(total)
        spare = ext_ref.at[s]
        spare[0:1] = value[0:1] * note[4 + tr_dev]
        for i in range(tr_dev):
            at = line_at(i * tile, tile)
            spare[1 + i * tile : 1 + (i + 1) * tile] = value[at : at + tile] * note[4 + i]
        spare[height + 1 : height + 2] = value[lines - 1 : lines] * note[5 + tr_dev]
        put_pads(t_ref.at[0], [], spare, 0, flags, [], flip, tile)
        z_ref = (zw2_ref, ze2_ref)[s]
        z_ref[0:lines] = tall_conv(t_ref.at[0], k2_ref, 2 * s, lines)

    x_ref[0] = north_ref[width : 2 * width]
    x_ref[height + 1] = south_ref[0:width]
    for i in range(tr_dev):
        loads[i].wait()
        for j in range(tc_dev):
            scale = jnp.full((1, ch), 1.0, F32) * wet_ref[i * tc_dev + j].astype(F32)
            m_ref[i, j * tile : (j + 1) * tile] = jnp.broadcast_to(scale, (tile, ch))
            x_ref[1 + i * tile : 1 + (i + 1) * tile, j * tile : (j + 1) * tile] = (
                out_ref[i, j] * scale.astype(BF16)[None]
            )

    beyond = (
        (0, [north_ref[0:width], north_ref[width : 2 * width], x_ref[1]], 0, notes[0]),
        (height + 1, [x_ref[height], south_ref[0:width], south_ref[width : 2 * width]], lines - 1, notes[1]),
    )
    for row, window, line, note in beyond:
        z = dot(jnp.concatenate(window, axis=1), w1_ref[: 3 * ch, : 3 * ch])
        total = side_sums(z, 0, zw1_ref[line : line + 1], ze1_ref[line : line + 1]) + bias1
        value = gelu(total)
        for j in range(tc_dev):
            hid_ref[row, j * tile : (j + 1) * tile] = (
                value[j * tile : (j + 1) * tile] * note[4 + j : 5 + j]
            ).astype(BF16)

    def first(p, carry):
        row = 2 * p
        window = [x_ref[row + k] for k in range(4)]
        outs = conv_pair(window, w1_ref, bias1, zw1_ref, ze1_ref, line_at(row, tile))
        for ro in range(2):
            hid_ref[1 + row + ro] = (gelu(outs[ro]) * m_ref[row // tile]).astype(BF16)
        return carry

    def second(p, carry):
        row = 2 * p
        i = row // tile
        inner = row % tile
        window = [hid_ref[row + k] for k in range(4)]
        outs = conv_pair(window, w2_ref, bias2, zw2_ref, ze2_ref, line_at(row, tile))
        branch = jnp.concatenate([gelu(o).astype(BF16) for o in outs], axis=1)
        mixed = dot(branch, mm_ref[...])
        for ro in range(2):
            own = out_ref[i, :, inner + ro].reshape(width, ch).astype(F32)
            total = (own + mixed[:, ro * ch : (ro + 1) * ch]).astype(BF16)
            out_ref[i, :, inner + ro] = total.reshape(tc_dev, tile, ch)
        return carry

    def copies(i, act):
        for j in range(tc_dev):
            k = i * tc_dev + j
            target = dst_ref[k]

            @pl.when((target >= 0) & (target < slots))
            def _():
                act(pltpu.make_async_copy(out_ref.at[i, j], keep_ref.at[target], sems.at[k]))

            @pl.when(target >= slots)
            def _():
                act(pltpu.make_async_copy(out_ref.at[i, j], give_ref.at[target - slots], sems.at[k]))

    lax.fori_loop(0, height // 2, first, 0, unroll=4)
    for i in range(tr_dev):
        lax.fori_loop(i * tile // 2, (i + 1) * tile // 2, second, 0, unroll=4)
        copies(i, lambda c: c.start())
    for i in range(tr_dev):
        copies(i, lambda c: c.wait())


def scatter_kernel(dst_ref, src_ref, held_ref, out_ref, buf_ref, in_sems, sems):
    def each(act):
        for k in range(src_ref.shape[0]):

            @pl.when(dst_ref[k] >= 0)
            def _():
                act(k)

    def load(k):
        return pltpu.make_async_copy(src_ref.at[k], buf_ref.at[k], in_sems.at[k])

    def store(k):
        return pltpu.make_async_copy(buf_ref.at[k], out_ref.at[dst_ref[k]], sems.at[k])

    def turn(k):
        load(k).wait()
        store(k).start()

    each(lambda k: load(k).start())
    each(turn)
    each(lambda k: store(k).wait())


def gather_kernel(idx_ref, src_ref, out_ref, buf_ref, in_sems, sems):
    count = out_ref.shape[0]

    def load(k):
        return pltpu.make_async_copy(src_ref.at[idx_ref[k]], buf_ref.at[k], in_sems.at[k])

    def store(k):
        return pltpu.make_async_copy(buf_ref.at[k], out_ref.at[k], sems.at[k])

    for k in range(count):
        load(k).start()
    for k in range(count):
        load(k).wait()
        store(k).start()
    for k in range(count):
        store(k).wait()


def shifted(x, axis, step):
    count = lax.axis_size(axis)
    pairs = [(i, i + step) for i in range(count) if 0 <= i + step < count]
    return lax.ppermute(x, axis, pairs)


def side_pack(north, south, columns, at, wets):
    width = (north.shape[0] - 16) // 2
    tc_dev = 8
    filler = jnp.zeros((4, north.shape[1]), north.dtype)
    pieces = []
    for n in range(2):
        c = at + n
        pieces += [north[c : c + 1], north[width + c : width + c + 1], columns[n]]
        pieces += [south[c : c + 1], south[width + c : width + c + 1], filler]
    side = 1 if at else 0
    tile = at and tc_dev - 1
    base = 2 * width
    pieces += [ref[base + 2 * side : base + 2 * side + 2] for ref in (north, south)]
    pieces += wets
    pieces += [ref[base + 4 + tile : base + 5 + tile] for ref in (north, south)]
    pieces.append(jnp.zeros((8, north.shape[1]), north.dtype))
    return jnp.concatenate(pieces, axis=0)


def on_device(
    fields, wet_mask, seam_flags, wet_list, kernel_one, bias_one, kernel_two, bias_two, mixing
):
    tr_dev, tc_dev, tile, _, ch = fields.shape
    face = tr_dev * tc_dev
    wet_dev = wet_list.shape[0]
    columns = lax.axis_size("col")
    chips = columns // 2
    width, height = tc_dev * tile, tr_dev * tile
    me = lax.axis_index("col")
    core = me % 2
    wet = wet_mask.reshape(face)
    flags = jnp.stack([seam_flags[:, 0, 0], seam_flags[:, tc_dev - 1, 1]], axis=1).reshape(-1)

    total = jnp.broadcast_to(jnp.sum(wet), (columns, 1, 1))
    counts = lax.all_to_all(total, "col", split_axis=0, concat_axis=0, tiled=True).reshape(columns)
    cids = jnp.arange(columns)
    start = jnp.sum(jnp.where(cids < me, counts, 0))
    mate = me ^ 1
    mate_start = jnp.sum(jnp.where(cids < mate, counts, 0))
    mate_count = jnp.sum(jnp.where(cids == mate, counts, 0))
    ids = jnp.arange(face)
    local = jnp.sum(jnp.where(ids[None, :] < ids[:, None], wet[None, :], 0), axis=1)
    rank = start + local
    slot = (rank % columns) // 2
    dst = jnp.where(wet == 1, jnp.where(rank % 2 == core, slot, chips + local // 2), -1)
    half = face // 2
    mate_local = 2 * jnp.arange(half) + (mate_start + core) % 2
    mate_dst = jnp.where(mate_local < mate_count, ((mate_start + mate_local) % columns) // 2, -1)
    source_chip = (wet_list % (tc_dev * columns)) // (2 * tc_dev)

    params = pltpu.CompilerParams(vmem_limit_bytes=VMEM_LIMIT)
    strip = jax.ShapeDtypeStruct((2 * width + 16, ch), BF16)
    pair = jax.ShapeDtypeStruct((2, height, ch), BF16)
    top, bottom, lcols, rcols = pl.pallas_call(
        rim_kernel,
        out_shape=(strip, strip, pair, pair),
        in_specs=[SCALARS, SCALARS, IN_PLACE],
        out_specs=(WHOLE,) * 4,
        scratch_shapes=[
            pltpu.VMEM((2, tc_dev, 2, tile, ch), BF16),
            pltpu.VMEM((2, tr_dev, tile, 16, ch), BF16),
            pltpu.VMEM((2, height * 16, ch), F32),
            pltpu.SemaphoreType.DMA((4,)),
        ],
        name="rim",
    )(wet, flags, fields)
    north = shifted(bottom, "row", 1)
    south = shifted(top, "row", -1)
    wets = jnp.broadcast_to(wet_mask.astype(BF16)[:, :, None, None], (tr_dev, tc_dev, 1, ch))
    west = shifted(
        side_pack(north, south, rcols, width - 2, [wets[i, -1] for i in range(tr_dev)]), "col", 1
    )
    east = shifted(side_pack(north, south, lcols, 0, [wets[i, 0] for i in range(tr_dev)]), "col", -1)

    tile_shape = (tile, tile, ch)
    lines = 8 + (tile + 2) * tr_dev
    lines += -lines % 8
    keep, give = pl.pallas_call(
        conv_kernel,
        out_shape=(
            jax.ShapeDtypeStruct((chips,) + tile_shape, BF16),
            jax.ShapeDtypeStruct((half,) + tile_shape, BF16),
        ),
        in_specs=[SCALARS] * 3 + [IN_PLACE] + [WHOLE] * 11,
        out_specs=(IN_PLACE, IN_PLACE),
        scratch_shapes=[
            pltpu.VMEM(fields.shape, BF16),
            pltpu.VMEM((height + 2, width, ch), BF16),
            pltpu.VMEM((height + 2, width, ch), BF16),
            pltpu.VMEM((4 * ch, 6 * ch), BF16),
            pltpu.VMEM((4 * ch, 6 * ch), BF16),
            pltpu.VMEM((2 * ch, 2 * ch), BF16),
            pltpu.VMEM((tr_dev, width, ch), F32),
            pltpu.VMEM((2,) + west.shape, F32),
            pltpu.VMEM((2, height + 8, ch), F32),
            pltpu.VMEM((2, height + 8, ch), F32),
            pltpu.VMEM((4, lines, ch), F32),
            pltpu.VMEM((lines, ch), F32),
            pltpu.VMEM((lines, ch), F32),
            pltpu.VMEM((lines, ch), F32),
            pltpu.VMEM((lines, ch), F32),
            pltpu.SemaphoreType.DMA((tr_dev,)),
            pltpu.SemaphoreType.DMA((face,)),
        ],
        compiler_params=params,
        name="both_convs",
    )(
        wet, flags, dst, fields, north, south, west, east, lcols[0], rcols[1],
        kernel_one, bias_one[None], kernel_two, bias_two[None], mixing,
    )

    taken = lax.ppermute(give, "col", [(i, i ^ 1) for i in range(columns)])
    sending = pl.pallas_call(
        scatter_kernel,
        out_shape=jax.ShapeDtypeStruct(keep.shape, BF16),
        in_specs=[SCALARS, IN_PLACE, IN_PLACE],
        out_specs=IN_PLACE,
        scratch_shapes=[
            pltpu.VMEM((half,) + tile_shape, BF16),
            pltpu.SemaphoreType.DMA((half,)),
            pltpu.SemaphoreType.DMA((half,)),
        ],
        input_output_aliases={2: 0},
        name="merge_mate",
    )(mate_dst, taken, keep)
    groups = [[2 * k + c for k in range(chips)] for c in range(2)]
    arrived = lax.all_to_all(
        sending, "col", split_axis=0, concat_axis=0, tiled=True, axis_index_groups=groups
    )
    return pl.pallas_call(
        gather_kernel,
        out_shape=jax.ShapeDtypeStruct((wet_dev,) + tile_shape, BF16),
        in_specs=[SCALARS, IN_PLACE],
        out_specs=IN_PLACE,
        scratch_shapes=[
            pltpu.VMEM((wet_dev,) + tile_shape, BF16),
            pltpu.SemaphoreType.DMA((wet_dev,)),
            pltpu.SemaphoreType.DMA((wet_dev,)),
        ],
        name="slot_order",
    )(source_chip, arrived)


def solution(mesh):
    return jax.shard_map(
        on_device,
        mesh=mesh,
        in_specs=(
            P("row", "col", None, None, None),
            P("row", "col"),
            P("row", "col", None),
            P(("row", "col")),
            P(),
            P(),
            P(),
            P(),
            P(),
        ),
        out_specs=P(("row", "col"), None, None, None),
        check_vma=False,
    )
```

```python
import functools

import jax
import jax.numpy as jnp
from jax import lax
from jax.experimental import pallas as pl
from jax.experimental.pallas import tpu as pltpu
from jax.sharding import PartitionSpec as P

F32 = jnp.float32
BF16 = jnp.bfloat16
VMEM_LIMIT = 32 * 1024 * 1024
WHOLE = pl.BlockSpec(memory_space=pltpu.VMEM)
SCALARS = pl.BlockSpec(memory_space=pltpu.SMEM)
IN_PLACE = pl.BlockSpec(memory_space=pl.ANY)
IN_HBM = pl.BlockSpec(memory_space=pltpu.HBM)


def dot(a, b):
    return jnp.dot(a, b, preferred_element_type=F32)


def gelu(x):
    u = x * (0.7978845608028654 + 0.03567740813636141 * (x * x))
    half = 0.5 * x
    return half + half * jnp.tanh(u)


def fill_weights(k_ref, w_ref):
    ch = k_ref.shape[2]
    zero = jnp.zeros((ch, 3 * ch), BF16)
    w_ref[3 * ch :, : 3 * ch] = zero
    w_ref[:ch, 3 * ch :] = zero
    for dy in range(3):
        for dx in range(3):
            block = k_ref[dy, dx]
            w_ref[dy * ch : (dy + 1) * ch, dx * ch : (dx + 1) * ch] = block
            w_ref[(dy + 1) * ch : (dy + 2) * ch, (3 + dx) * ch : (4 + dx) * ch] = block


def tall_conv(t_ref, k_ref, dx, count):
    total = dot(t_ref[0:count].astype(BF16), k_ref[0, dx])
    total += dot(t_ref[1 : count + 1].astype(BF16), k_ref[1, dx])
    total += dot(t_ref[2 : count + 2].astype(BF16), k_ref[2, dx])
    return total


def put_columns(t_ref, col_ref, base, tr_dev, tile):
    tall = tile + 2
    t_ref[0:3] = col_ref[base : base + 3]
    for i in range(tr_dev):
        t_ref[3 + tall * i : 3 + tall * (i + 1)] = col_ref[
            base + 1 + tile * i : base + 1 + tile * i + tall
        ]
    last = 3 + tall * tr_dev
    t_ref[last : last + 3] = col_ref[base + 1 + tile * tr_dev : base + 4 + tile * tr_dev]


def put_pads(t_ref, above, ext_ref, base, flags, below, flip, tile):
    tall = tile + 2
    for n, line in enumerate(above):
        t_ref[n : n + 1] = line
    for i, flag in enumerate(flags):
        at = 3 + tall * i
        from_row = base + tile * i
        t_ref[at : at + 1] = ext_ref[from_row : from_row + 1]
        middle = ext_ref[from_row + 1 : from_row + 1 + tile]
        turned = dot(flip, middle.astype(BF16))
        t_ref[at + 1 : at + 1 + tile] = jnp.where(flag > 0.5, turned, middle)
        t_ref[at + tall - 1 : at + tall] = ext_ref[from_row + tile + 1 : from_row + tile + 2]
    last = 3 + tall * len(flags)
    for n, line in enumerate(below):
        t_ref[last + n : last + n + 1] = line


def line_at(tall_row, tile):
    return 3 + tall_row + 2 * (tall_row // tile)


def side_sums(z, taps, west, east):
    ch = west.shape[1]
    width = z.shape[0]
    lane_row = lax.broadcasted_iota(jnp.int32, (8, ch), 0)
    left = pltpu.roll(z[:, taps : taps + ch], 1, 0)
    right = pltpu.roll(z[:, taps + 2 * ch : taps + 3 * ch], width - 1, 0)
    left = jnp.concatenate([jnp.where(lane_row == 0, west, left[:8]), left[8:]], axis=0)
    right = jnp.concatenate(
        [right[: width - 8], jnp.where(lane_row == 7, east, right[width - 8 :])], axis=0
    )
    return z[:, taps + ch : taps + 2 * ch] + left + right


def conv_pair(window, w_ref, bias, zw_ref, ze_ref, line):
    ch = window[0].shape[1]
    z = dot(jnp.concatenate(window, axis=1), w_ref[...])
    outs = []
    for ro in range(2):
        west = zw_ref[pl.ds(line + ro, 1), :]
        east = ze_ref[pl.ds(line + ro, 1), :]
        outs.append(side_sums(z, 3 * ro * ch, west, east) + bias)
    return outs


def seam_line(seam_ref, i, j, side, ch):
    return jnp.full((1, ch), 1.0, F32) * seam_ref[i, side, j].astype(F32)


def rim_kernel(
    wet_ref, seam_ref, fields_ref, top_ref, bottom_ref, lcol_ref, rcol_ref, count_ref,
    rows_ref, cols_ref, line_ref, sems,
):
    tr_dev, tc_dev, tile, _, ch = fields_ref.shape
    width, height = tc_dev * tile, tr_dev * tile
    part = cols_ref.shape[3]
    loads = [
        pltpu.make_async_copy(fields_ref.at[0, :, 0:2], rows_ref.at[0], sems.at[0]),
        pltpu.make_async_copy(fields_ref.at[tr_dev - 1, :, tile - 2 : tile], rows_ref.at[1], sems.at[1]),
        pltpu.make_async_copy(fields_ref.at[:, 0, :, 0:part], cols_ref.at[0], sems.at[2]),
        pltpu.make_async_copy(fields_ref.at[:, tc_dev - 1, :, tile - part :], cols_ref.at[1], sems.at[3]),
    ]
    for load in loads:
        load.start()

    def wet(i, j):
        return jnp.full((1, ch), 1.0, F32) * wet_ref[i, j].astype(F32)

    total = sum(wet_ref[i, j] for i in range(tr_dev) for j in range(tc_dev))
    count_ref[...] = jnp.full(count_ref.shape, 1.0, F32) * total.astype(F32)
    for load in loads:
        load.wait()
    for side, (out_ref, i) in enumerate(((top_ref, 0), (bottom_ref, tr_dev - 1))):
        for j in range(tc_dev):
            scale = wet(i, j).astype(BF16)
            for n in range(2):
                out_ref[n * width + j * tile : n * width + (j + 1) * tile] = (
                    rows_ref[side, j, n] * scale
                )
    picked = []
    for side, out_ref in enumerate((lcol_ref, rcol_ref)):
        for i in range(tr_dev):
            block = cols_ref[side, i].astype(F32) * wet(i, side * (tc_dev - 1))[None]
            line_ref[side, i * tile * part : (i + 1) * tile * part] = block.reshape(tile * part, ch)
        first = side * (part - 2)
        columns = [line_ref[side, pl.ds(first + n, height, stride=part)] for n in range(2)]
        out_ref[0] = columns[0].astype(BF16)
        out_ref[1] = columns[1].astype(BF16)
        picked.append(columns[side])
    for out_ref, i, near in ((top_ref, 0, tile - 2), (bottom_ref, tr_dev - 1, tile * (tr_dev - 1))):
        extra = [column[near : near + 2] for column in picked]
        extra += [wet(i, j) for j in range(tc_dev)]
        extra += [
            seam_line(seam_ref, i, side * (tc_dev - 1), side, ch) for side in range(2)
        ]
        extra.append(jnp.zeros((12 - tc_dev - 2, ch), F32))
        at = 0
        for piece in extra:
            line_ref[0, at : at + piece.shape[0]] = piece
            at += piece.shape[0]
        out_ref[2 * width : 2 * width + 16] = line_ref[0, 0:16].astype(BF16)


def pixel(ref, n):
    base = n // 16 * 16
    return ref[base : base + 16].astype(F32)[n - base : n - base + 1]


def side_kernel(wet_ref, north_ref, south_ref, lcol_ref, rcol_ref, left_ref, right_ref, line_ref):
    tr_dev, tc_dev = wet_ref.shape
    ch = north_ref.shape[1]
    height = lcol_ref.shape[1]
    width = (north_ref.shape[0] - 16) // 2
    span = height + 8
    notes = [ref[2 * width : 2 * width + 16].astype(F32) for ref in (north_ref, south_ref)]
    for s, (out_ref, own) in enumerate(((left_ref, lcol_ref), (right_ref, rcol_ref))):
        for n in range(2):
            c = s * (width - 2) + n
            at = n * span
            line_ref[at : at + 1] = pixel(north_ref, c)
            line_ref[at + 1 : at + 2] = pixel(north_ref, width + c)
            line_ref[at + 2 : at + 2 + height] = own[n].astype(F32)
            line_ref[at + 2 + height : at + 3 + height] = pixel(south_ref, c)
            line_ref[at + 3 + height : at + 4 + height] = pixel(south_ref, width + c)
            line_ref[at + 4 + height : at + span] = jnp.zeros((4, ch), F32)
        at = 2 * span
        j = s * (tc_dev - 1)
        line_ref[at : at + 16] = jnp.zeros((16, ch), F32)
        line_ref[at : at + 2] = notes[0][2 * s : 2 * s + 2]
        line_ref[at + 2 : at + 4] = notes[1][2 * s : 2 * s + 2]
        for i in range(tr_dev):
            line_ref[at + 4 + i : at + 5 + i] = jnp.full((1, ch), 1.0, F32) * wet_ref[i, j].astype(F32)
        line_ref[at + 4 + tr_dev : at + 5 + tr_dev] = notes[0][4 + j : 5 + j]
        line_ref[at + 5 + tr_dev : at + 6 + tr_dev] = notes[1][4 + j : 5 + j]
        out_ref[...] = line_ref[...].astype(BF16)


def wet_before(count_ref, place):
    row = lax.broadcasted_iota(jnp.int32, count_ref.shape, 0)
    earlier = jnp.where(row < place, count_ref[...], 0.0)
    return jnp.max(jnp.sum(earlier, axis=0)).astype(jnp.int32)


def conv_kernel(
    wet_ref, seam_ref, count_ref, fields_ref, north_ref, south_ref, west_ref, east_ref,
    lcol_ref, rcol_ref, k1_ref, b1_ref, k2_ref, b2_ref, mix_ref, keep_ref, give_ref,
    own_tiles, out_ref, x_ref, hid_ref, br_ref, w1_ref, w2_ref, mm_ref, m_ref, pack_ref, own_ref, ext_ref, t_ref,
    zw1_ref, ze1_ref, zw2_ref, ze2_ref, in_sems, sems,
):
    tr_dev, tc_dev, tile, _, ch = fields_ref.shape
    width, height = tc_dev * tile, tr_dev * tile
    slots = keep_ref.shape[0]
    tall = 3 + (tile + 2) * tr_dev + 3
    lines = tall - 2
    loads = [
        pltpu.make_async_copy(fields_ref.at[i], own_tiles.at[i], in_sems.at[i]) for i in range(tr_dev)
    ]
    for load in loads:
        load.start()
    fill_weights(k1_ref, w1_ref)
    fill_weights(k2_ref, w2_ref)
    zero = jnp.zeros((ch, ch), BF16)
    mm_ref[:ch, :ch] = mix_ref[...]
    mm_ref[ch:, ch:] = mix_ref[...]
    mm_ref[:ch, ch:] = zero
    mm_ref[ch:, :ch] = zero
    bias1 = b1_ref[...]
    bias2 = b2_ref[...]
    rows = lax.broadcasted_iota(jnp.int32, (tile, tile), 0)
    cols = lax.broadcasted_iota(jnp.int32, (tile, tile), 1)
    flip = jnp.where(rows + cols == tile - 1, 1.0, 0.0).astype(BF16)

    notes = [ref[2 * width : 2 * width + 16].astype(F32) for ref in (north_ref, south_ref)]
    flagged = [[note[4 + tc_dev + s : 5 + tc_dev + s] > 0.5 for s in range(2)] for note in notes]

    step_size = height + 8
    sides = ((west_ref, lcol_ref.at[0], 0), (east_ref, rcol_ref.at[1], width - 1))
    for s, (pack, own, c) in enumerate(sides):
        pack_ref[s] = pack[...].astype(F32)
        own_ref[s, 1 : height + 1] = own[...].astype(F32)
        own_ref[s, 0:1] = pixel(north_ref, width + c)
        own_ref[s, height + 1 : height + 2] = pixel(south_ref, c)
    for s, (pack, own, c) in enumerate(sides):
        near = step_size * (1 - s)
        far = step_size * s
        notes_at = 2 * step_size
        note = [pack_ref[s, notes_at + n : notes_at + n + 1] for n in range(8)]
        held = pack_ref.at[s]
        mine = own_ref.at[s]
        flags = [seam_line(seam_ref, i, s * (tc_dev - 1), s, ch) for i in range(tr_dev)]
        north_flag, south_flag = flagged[0][s], flagged[1][s]

        def near_line(n, near=near, held=held):
            return held[near + n : near + n + 1]

        above = [
            jnp.where(north_flag, note[1], near_line(0)),
            jnp.where(north_flag, note[0], near_line(1)),
            near_line(2),
        ]
        below = [
            near_line(height + 1),
            jnp.where(south_flag, note[3], near_line(height + 2)),
            jnp.where(south_flag, note[2], near_line(height + 3)),
        ]
        put_pads(t_ref.at[0], above, held, near + 1, flags, below, flip, tile)
        z_ref = (zw1_ref, ze1_ref)[s]
        z_ref[0:lines] = tall_conv(t_ref.at[0], k1_ref, 2 * s, lines)
        total = bias1
        put_columns(t_ref.at[1], held, near, tr_dev, tile)
        total = total + tall_conv(t_ref.at[1], k1_ref, 1, lines)
        put_columns(t_ref.at[2], held, far, tr_dev, tile)
        total = total + tall_conv(t_ref.at[2], k1_ref, 2 * s, lines)
        above = [
            jnp.where(north_flag, notes[0][2 * s + 1 : 2 * s + 2], pixel(north_ref, c)),
            jnp.where(north_flag, notes[0][2 * s : 2 * s + 1], pixel(north_ref, width + c)),
            mine[1:2],
        ]
        below = [
            mine[height : height + 1],
            jnp.where(south_flag, notes[1][2 * s + 1 : 2 * s + 2], pixel(south_ref, c)),
            jnp.where(south_flag, notes[1][2 * s : 2 * s + 1], pixel(south_ref, width + c)),
        ]
        put_pads(t_ref.at[3], above, mine, 0, flags, below, flip, tile)
        total = total + tall_conv(t_ref.at[3], k1_ref, 2 - 2 * s, lines)
        value = gelu(total)
        spare = ext_ref.at[s]
        spare[0:1] = value[0:1] * note[4 + tr_dev]
        for i in range(tr_dev):
            at = line_at(i * tile, tile)
            spare[1 + i * tile : 1 + (i + 1) * tile] = value[at : at + tile] * note[4 + i]
        spare[height + 1 : height + 2] = value[lines - 1 : lines] * note[5 + tr_dev]
        put_pads(t_ref.at[0], [], spare, 0, flags, [], flip, tile)
        z_ref = (zw2_ref, ze2_ref)[s]
        z_ref[0:lines] = tall_conv(t_ref.at[0], k2_ref, 2 * s, lines)

    x_ref[0] = north_ref[width : 2 * width]
    x_ref[height + 1] = south_ref[0:width]

    def fill(i):
        loads[i].wait()
        for j in range(tc_dev):
            scale = jnp.full((1, ch), 1.0, F32) * wet_ref[i, j].astype(F32)
            m_ref[i, j * tile : (j + 1) * tile] = jnp.broadcast_to(scale, (tile, ch))
            x_ref[1 + i * tile : 1 + (i + 1) * tile, j * tile : (j + 1) * tile] = (
                own_tiles[i, j] * scale.astype(BF16)[None]
            )

    beyond = (
        (0, [north_ref.at[0:width], north_ref.at[width : 2 * width], x_ref.at[1]], 0, notes[0]),
        (height + 1, [x_ref.at[height], south_ref.at[0:width], south_ref.at[width : 2 * width]], lines - 1, notes[1]),
    )

    def outside(row, window, line, note):
        window = [w[...] for w in window]
        z = dot(jnp.concatenate(window, axis=1), w1_ref[: 3 * ch, : 3 * ch])
        total = side_sums(z, 0, zw1_ref[line : line + 1], ze1_ref[line : line + 1]) + bias1
        value = gelu(total)
        for j in range(tc_dev):
            hid_ref[row, j * tile : (j + 1) * tile] = (
                value[j * tile : (j + 1) * tile] * note[4 + j : 5 + j]
            ).astype(BF16)

    def first(p, carry):
        row = 2 * p
        window = [x_ref[row + k] for k in range(4)]
        outs = conv_pair(window, w1_ref, bias1, zw1_ref, ze1_ref, line_at(row, tile))
        for ro in range(2):
            hid_ref[1 + row + ro] = (gelu(outs[ro]) * m_ref[row // tile]).astype(BF16)
        return carry

    def branch(p):
        row = 2 * p
        window = [hid_ref[row + k] for k in range(4)]
        outs = conv_pair(window, w2_ref, bias2, zw2_ref, ze2_ref, line_at(row, tile))
        for ro in range(2):
            br_ref[p, :, ro * ch : (ro + 1) * ch] = gelu(outs[ro]).astype(BF16)

    def mix(p):
        i = 2 * p // tile
        inner = 2 * p % tile
        mixed = dot(br_ref[p], mm_ref[...])
        for ro in range(2):
            own = own_tiles[i, :, inner + ro].reshape(width, ch).astype(F32)
            total = (own + mixed[:, ro * ch : (ro + 1) * ch]).astype(BF16)
            out_ref[i, :, inner + ro] = total.reshape(tc_dev, tile, ch)

    def second(p, carry):
        branch(p)
        return carry

    def third(p, carry):
        mix(p)
        return carry

    place = lax.axis_index("col")
    rank = wet_before(count_ref, place)
    odd = place % 2
    targets = []
    given = 0
    for i in range(tr_dev):
        for j in range(tc_dev):
            kept = rank % 2 == odd
            slot = jnp.where(kept, rank % (2 * slots) // 2, slots + given // 2)
            targets.append(jnp.where(wet_ref[i, j] == 1, slot, -1))
            rank += wet_ref[i, j]
            given += wet_ref[i, j]

    def start_copies(i):
        for j in range(tc_dev):
            k = i * tc_dev + j
            target = targets[k]

            @pl.when((target >= 0) & (target < slots))
            def _():
                pltpu.make_async_copy(out_ref.at[i, j], keep_ref.at[target], sems.at[k]).start()

            @pl.when(target >= slots)
            def _():
                pltpu.make_async_copy(
                    out_ref.at[i, j], give_ref.at[target - slots], sems.at[k]
                ).start()

    def wait_copies(i):
        for j in range(tc_dev):
            k = i * tc_dev + j

            @pl.when(wet_ref[i, j] == 1)
            def _():
                pltpu.make_async_copy(out_ref.at[i, j], keep_ref.at[0], sems.at[k]).wait()

    done = 0
    for i in range(tr_dev):
        fill(i)
        if i == 0:
            outside(*beyond[0])
        if i == tr_dev - 1:
            outside(*beyond[1])
        ready = (i + 1) * tile // 2 - (i < tr_dev - 1)
        lax.fori_loop(done, ready, first, 0, unroll=ready - done)
        done = ready
    for i in range(tr_dev):
        lax.fori_loop(i * tile // 2, (i + 1) * tile // 2, second, 0, unroll=tile // 2)
        lax.fori_loop(i * tile // 2, (i + 1) * tile // 2, third, 0, unroll=8)
        start_copies(i)
    for i in range(tr_dev):
        wait_copies(i)


def scatter_kernel(count_ref, src_ref, held_ref, out_ref, sems):
    slots = out_ref.shape[0]
    place = lax.axis_index("col")
    odd = place % 2
    mate = place + 1 - 2 * odd
    start = wet_before(count_ref, mate)
    stop = wet_before(count_ref, mate + 1)
    ranks = [start + 2 * k + (start + odd) % 2 for k in range(src_ref.shape[0])]

    def each(act):
        for k, rank in enumerate(ranks):

            @pl.when(rank < stop)
            def _():
                act(k)

    def store(k):
        slot = ranks[k] % (2 * slots) // 2
        return pltpu.make_async_copy(src_ref.at[k], out_ref.at[slot], sems.at[k])

    each(lambda k: store(k).start())
    each(lambda k: store(k).wait())


def gather_kernel(across, list_ref, src_ref, out_ref, sems):
    chips = src_ref.shape[0]
    copies = []
    for k in range(out_ref.shape[0]):
        chip = list_ref[k] % across // (across // chips)
        copies.append(pltpu.make_async_copy(src_ref.at[chip], out_ref.at[k], sems.at[k]))
    for copy in copies:
        copy.start()
    for copy in copies:
        copy.wait()


def shifted(x, axis, step):
    count = lax.axis_size(axis)
    pairs = [(i, i + step) for i in range(count) if 0 <= i + step < count]
    return lax.ppermute(x, axis, pairs)


def on_device(
    fields, wet_mask, seam_flags, wet_list, kernel_one, bias_one, kernel_two, bias_two, mixing
):
    tr_dev, tc_dev, tile, _, ch = fields.shape
    face = tr_dev * tc_dev
    wet_dev = wet_list.shape[0]
    columns = lax.axis_size("col")
    chips = columns // 2
    width, height = tc_dev * tile, tr_dev * tile
    half = face // 2
    seams = jnp.swapaxes(seam_flags, 1, 2)
    params = pltpu.CompilerParams(vmem_limit_bytes=VMEM_LIMIT)
    small = pltpu.CompilerParams(vmem_limit_bytes=VMEM_LIMIT // 8)
    fields = pltpu.with_memory_space_constraint(fields, pltpu.HBM)
    strip = jax.ShapeDtypeStruct((2 * width + 16, ch), BF16)
    pair = jax.ShapeDtypeStruct((2, height, ch), BF16)
    top, bottom, lcols, rcols, count = pl.pallas_call(
        rim_kernel,
        out_shape=(strip, strip, pair, pair, jax.ShapeDtypeStruct((columns, 1, ch), F32)),
        in_specs=[SCALARS, SCALARS, IN_HBM],
        out_specs=(WHOLE,) * 5,
        scratch_shapes=[
            pltpu.VMEM((2, tc_dev, 2, tile, ch), BF16),
            pltpu.VMEM((2, tr_dev, tile, 16, ch), BF16),
            pltpu.VMEM((2, height * 16, ch), F32),
            pltpu.SemaphoreType.DMA((4,)),
        ],
        compiler_params=small,
        name="rim",
    )(wet_mask, seams, fields)
    north = shifted(bottom, "row", 1)
    south = shifted(top, "row", -1)
    counts = lax.all_to_all(count, "col", split_axis=0, concat_axis=0, tiled=True)
    pack = jax.ShapeDtypeStruct((2 * (height + 8) + 16, ch), BF16)
    left, right = pl.pallas_call(
        side_kernel,
        out_shape=(pack, pack),
        in_specs=[SCALARS] + [WHOLE] * 4,
        out_specs=(WHOLE,) * 2,
        scratch_shapes=[pltpu.VMEM(pack.shape, F32)],
        compiler_params=small,
        name="side",
    )(wet_mask, north, south, lcols, rcols)
    left, right, counts = lax.optimization_barrier((left, right, counts))
    west = shifted(right, "col", 1)
    east = shifted(left, "col", -1)

    tile_shape = (tile, tile, ch)
    lines = 8 + (tile + 2) * tr_dev
    lines += -lines % 8
    keep, give = pl.pallas_call(
        conv_kernel,
        out_shape=(
            jax.ShapeDtypeStruct((chips,) + tile_shape, BF16),
            jax.ShapeDtypeStruct((half,) + tile_shape, BF16),
        ),
        in_specs=[SCALARS, SCALARS, WHOLE, IN_HBM] + [WHOLE] * 11,
        out_specs=(IN_PLACE, IN_PLACE),
        scratch_shapes=[
            pltpu.VMEM(fields.shape, BF16),
            pltpu.VMEM(fields.shape, BF16),
            pltpu.VMEM((height + 2, width, ch), BF16),
            pltpu.VMEM((height + 2, width, ch), BF16),
            pltpu.VMEM((height // 2, width, 2 * ch), BF16),
            pltpu.VMEM((4 * ch, 6 * ch), BF16),
            pltpu.VMEM((4 * ch, 6 * ch), BF16),
            pltpu.VMEM((2 * ch, 2 * ch), BF16),
            pltpu.VMEM((tr_dev, width, ch), F32),
            pltpu.VMEM((2,) + west.shape, F32),
            pltpu.VMEM((2, height + 8, ch), F32),
            pltpu.VMEM((2, height + 8, ch), F32),
            pltpu.VMEM((4, lines, ch), F32),
            pltpu.VMEM((lines, ch), F32),
            pltpu.VMEM((lines, ch), F32),
            pltpu.VMEM((lines, ch), F32),
            pltpu.VMEM((lines, ch), F32),
            pltpu.SemaphoreType.DMA((tr_dev,)),
            pltpu.SemaphoreType.DMA((face,)),
        ],
        compiler_params=params,
        name="both_convs",
    )(
        wet_mask, seams, counts, fields, north, south, west, east, lcols, rcols,
        kernel_one, bias_one[None], kernel_two, bias_two[None], mixing,
    )

    taken = lax.ppermute(give, "col", [(i, i ^ 1) for i in range(columns)])
    sending = pl.pallas_call(
        scatter_kernel,
        out_shape=jax.ShapeDtypeStruct(keep.shape, BF16),
        in_specs=[WHOLE, WHOLE, IN_PLACE],
        out_specs=IN_PLACE,
        scratch_shapes=[pltpu.SemaphoreType.DMA((half,))],
        input_output_aliases={2: 0},
        compiler_params=small,
        name="merge_mate",
    )(counts, taken, keep)
    groups = [[2 * k + c for k in range(chips)] for c in range(2)]
    arrived = lax.all_to_all(
        sending, "col", split_axis=0, concat_axis=0, tiled=True, axis_index_groups=groups
    )
    return pl.pallas_call(
        functools.partial(gather_kernel, tc_dev * columns),
        out_shape=jax.ShapeDtypeStruct((wet_dev,) + tile_shape, BF16),
        in_specs=[SCALARS, WHOLE],
        out_specs=IN_HBM,
        scratch_shapes=[pltpu.SemaphoreType.DMA((wet_dev,))],
        compiler_params=small,
        name="slot_order",
    )(wet_list, arrived)


def solution(mesh):
    return jax.shard_map(
        on_device,
        mesh=mesh,
        in_specs=(
            P("row", "col", None, None, None),
            P("row", "col"),
            P("row", "col", None),
            P(("row", "col")),
            P(),
            P(),
            P(),
            P(),
            P(),
        ),
        out_specs=P(("row", "col"), None, None, None),
        check_vma=False,
    )
```

```python
import functools

import jax
import jax.numpy as jnp
from jax import lax
from jax.experimental import pallas as pl
from jax.experimental.pallas import tpu as pltpu
from jax.sharding import PartitionSpec as P

F32 = jnp.float32
BF16 = jnp.bfloat16
VMEM_LIMIT = 26 * 1024 * 1024
WHOLE = pl.BlockSpec(memory_space=pltpu.VMEM)
SCALARS = pl.BlockSpec(memory_space=pltpu.SMEM)
IN_PLACE = pl.BlockSpec(memory_space=pl.ANY)
IN_HBM = pl.BlockSpec(memory_space=pltpu.HBM)


def dot(a, b):
    return jnp.dot(a, b, preferred_element_type=F32)


def gelu(x):
    u = x * (0.7978845608028654 + 0.03567740813636141 * (x * x))
    half = 0.5 * x
    return half + half * jnp.tanh(u)


def fill_weights(k_ref, w_ref):
    ch = k_ref.shape[2]
    zero = jnp.zeros((ch, 3 * ch), BF16)
    w_ref[3 * ch :, : 3 * ch] = zero
    w_ref[:ch, 3 * ch :] = zero
    for dy in range(3):
        for dx in range(3):
            block = k_ref[dy, dx]
            w_ref[dy * ch : (dy + 1) * ch, dx * ch : (dx + 1) * ch] = block
            w_ref[(dy + 1) * ch : (dy + 2) * ch, (3 + dx) * ch : (4 + dx) * ch] = block


def tall_conv(t_ref, k_ref, dx, count):
    total = dot(t_ref[0:count].astype(BF16), k_ref[0, dx])
    total += dot(t_ref[1 : count + 1].astype(BF16), k_ref[1, dx])
    total += dot(t_ref[2 : count + 2].astype(BF16), k_ref[2, dx])
    return total


def put_columns(t_ref, col_ref, base, tr_dev, tile):
    tall = tile + 2
    t_ref[0:3] = col_ref[base : base + 3]
    for i in range(tr_dev):
        t_ref[3 + tall * i : 3 + tall * (i + 1)] = col_ref[
            base + 1 + tile * i : base + 1 + tile * i + tall
        ]
    last = 3 + tall * tr_dev
    t_ref[last : last + 3] = col_ref[base + 1 + tile * tr_dev : base + 4 + tile * tr_dev]


def put_pads(t_ref, above, ext_ref, base, flags, below, flip, tile):
    tall = tile + 2
    for n, line in enumerate(above):
        t_ref[n : n + 1] = line
    for i, flag in enumerate(flags):
        at = 3 + tall * i
        from_row = base + tile * i
        t_ref[at : at + 1] = ext_ref[from_row : from_row + 1]
        middle = ext_ref[from_row + 1 : from_row + 1 + tile]
        turned = dot(flip, middle.astype(BF16))
        t_ref[at + 1 : at + 1 + tile] = jnp.where(flag > 0.5, turned, middle)
        t_ref[at + tall - 1 : at + tall] = ext_ref[from_row + tile + 1 : from_row + tile + 2]
    last = 3 + tall * len(flags)
    for n, line in enumerate(below):
        t_ref[last + n : last + n + 1] = line


def line_at(tall_row, tile):
    return 3 + tall_row + 2 * (tall_row // tile)


def side_sums(z, taps, west, east):
    ch = west.shape[1]
    width = z.shape[0]
    lane_row = lax.broadcasted_iota(jnp.int32, (8, ch), 0)
    left = pltpu.roll(z[:, taps : taps + ch], 1, 0)
    right = pltpu.roll(z[:, taps + 2 * ch : taps + 3 * ch], width - 1, 0)
    left = jnp.concatenate([jnp.where(lane_row == 0, west, left[:8]), left[8:]], axis=0)
    right = jnp.concatenate(
        [right[: width - 8], jnp.where(lane_row == 7, east, right[width - 8 :])], axis=0
    )
    return z[:, taps + ch : taps + 2 * ch] + left + right


def conv_pair(window, w_ref, bias, zw_ref, ze_ref, line):
    ch = window[0].shape[1]
    z = dot(jnp.concatenate(window, axis=1), w_ref[...])
    outs = []
    for ro in range(2):
        west = zw_ref[pl.ds(line + ro, 1), :]
        east = ze_ref[pl.ds(line + ro, 1), :]
        outs.append(side_sums(z, 3 * ro * ch, west, east) + bias)
    return outs


def seam_line(seam_ref, i, j, side, ch):
    return jnp.full((1, ch), 1.0, F32) * seam_ref[i, side, j].astype(F32)


def rim_kernel(
    wet_ref, seam_ref, fields_ref, top_ref, bottom_ref, lcol_ref, rcol_ref, count_ref,
    rows_ref, cols_ref, line_ref, sems,
):
    tr_dev, tc_dev, tile, _, ch = fields_ref.shape
    width, height = tc_dev * tile, tr_dev * tile
    part = cols_ref.shape[3]
    loads = [
        pltpu.make_async_copy(fields_ref.at[0, :, 0:2], rows_ref.at[0], sems.at[0]),
        pltpu.make_async_copy(fields_ref.at[tr_dev - 1, :, tile - 2 : tile], rows_ref.at[1], sems.at[1]),
        pltpu.make_async_copy(fields_ref.at[:, 0, :, 0:part], cols_ref.at[0], sems.at[2]),
        pltpu.make_async_copy(fields_ref.at[:, tc_dev - 1, :, tile - part :], cols_ref.at[1], sems.at[3]),
    ]
    for load in loads:
        load.start()

    def wet(i, j):
        return jnp.full((1, ch), 1.0, F32) * wet_ref[i, j].astype(F32)

    total = sum(wet_ref[i, j] for i in range(tr_dev) for j in range(tc_dev))
    count_ref[...] = jnp.full(count_ref.shape, 1.0, F32) * total.astype(F32)
    for load in loads:
        load.wait()
    for side, (out_ref, i) in enumerate(((top_ref, 0), (bottom_ref, tr_dev - 1))):
        for j in range(tc_dev):
            scale = wet(i, j).astype(BF16)
            for n in range(2):
                out_ref[n * width + j * tile : n * width + (j + 1) * tile] = (
                    rows_ref[side, j, n] * scale
                )
    picked = []
    for side, out_ref in enumerate((lcol_ref, rcol_ref)):
        for i in range(tr_dev):
            block = cols_ref[side, i].astype(F32) * wet(i, side * (tc_dev - 1))[None]
            line_ref[side, i * tile * part : (i + 1) * tile * part] = block.reshape(tile * part, ch)
        first = side * (part - 2)
        columns = [line_ref[side, pl.ds(first + n, height, stride=part)] for n in range(2)]
        out_ref[0] = columns[0].astype(BF16)
        out_ref[1] = columns[1].astype(BF16)
        picked.append(columns[side])
    for out_ref, i, near in ((top_ref, 0, tile - 2), (bottom_ref, tr_dev - 1, tile * (tr_dev - 1))):
        extra = [column[near : near + 2] for column in picked]
        extra += [wet(i, j) for j in range(tc_dev)]
        extra += [
            seam_line(seam_ref, i, side * (tc_dev - 1), side, ch) for side in range(2)
        ]
        extra.append(jnp.zeros((12 - tc_dev - 2, ch), F32))
        at = 0
        for piece in extra:
            line_ref[0, at : at + piece.shape[0]] = piece
            at += piece.shape[0]
        out_ref[2 * width : 2 * width + 16] = line_ref[0, 0:16].astype(BF16)


def pixel(ref, n):
    base = n // 16 * 16
    return ref[base : base + 16].astype(F32)[n - base : n - base + 1]


def side_kernel(wet_ref, north_ref, south_ref, lcol_ref, rcol_ref, left_ref, right_ref, line_ref):
    tr_dev, tc_dev = wet_ref.shape
    ch = north_ref.shape[1]
    height = lcol_ref.shape[1]
    width = (north_ref.shape[0] - 16) // 2
    span = height + 8
    notes = [ref[2 * width : 2 * width + 16].astype(F32) for ref in (north_ref, south_ref)]
    for s, (out_ref, own) in enumerate(((left_ref, lcol_ref), (right_ref, rcol_ref))):
        for n in range(2):
            c = s * (width - 2) + n
            at = n * span
            line_ref[at : at + 1] = pixel(north_ref, c)
            line_ref[at + 1 : at + 2] = pixel(north_ref, width + c)
            line_ref[at + 2 : at + 2 + height] = own[n].astype(F32)
            line_ref[at + 2 + height : at + 3 + height] = pixel(south_ref, c)
            line_ref[at + 3 + height : at + 4 + height] = pixel(south_ref, width + c)
            line_ref[at + 4 + height : at + span] = jnp.zeros((4, ch), F32)
        at = 2 * span
        j = s * (tc_dev - 1)
        line_ref[at : at + 16] = jnp.zeros((16, ch), F32)
        line_ref[at : at + 2] = notes[0][2 * s : 2 * s + 2]
        line_ref[at + 2 : at + 4] = notes[1][2 * s : 2 * s + 2]
        for i in range(tr_dev):
            line_ref[at + 4 + i : at + 5 + i] = jnp.full((1, ch), 1.0, F32) * wet_ref[i, j].astype(F32)
        line_ref[at + 4 + tr_dev : at + 5 + tr_dev] = notes[0][4 + j : 5 + j]
        line_ref[at + 5 + tr_dev : at + 6 + tr_dev] = notes[1][4 + j : 5 + j]
        out_ref[...] = line_ref[...].astype(BF16)


def wet_before(count_ref, place):
    row = lax.broadcasted_iota(jnp.int32, count_ref.shape, 0)
    earlier = jnp.where(row < place, count_ref[...], 0.0)
    return jnp.max(jnp.sum(earlier, axis=0)).astype(jnp.int32)


def first_kernel(
    wet_ref, fields_ref, k_ref, b_ref, made_ref, col_ref, row_ref,
    own_tiles, x_ref, hid_ref, w_ref, m_ref, in_sems, out_sems,
):
    tr_dev, tc_dev, tile, _, ch = fields_ref.shape
    width, height = tc_dev * tile, tr_dev * tile
    loads = [
        pltpu.make_async_copy(fields_ref.at[i], own_tiles.at[i], in_sems.at[i])
        for i in range(tr_dev)
    ]
    for load in loads:
        load.start()
    fill_weights(k_ref, w_ref)
    bias = b_ref[...]
    x_ref[0] = jnp.zeros((width, ch), BF16)
    x_ref[height + 1] = jnp.zeros((width, ch), BF16)
    nothing = jnp.zeros((1, ch), F32)
    stores = []

    def store(n, row):
        rows = slice(row, row + tile // 2)
        return pltpu.make_async_copy(hid_ref.at[rows], made_ref.at[rows], out_sems.at[n])

    done = 0
    for i in range(tr_dev):
        loads[i].wait()
        for j in range(tc_dev):
            scale = jnp.full((1, ch), 1.0, F32) * wet_ref[i, j].astype(F32)
            m_ref[i, j * tile : (j + 1) * tile] = jnp.broadcast_to(scale, (tile, ch))
            x_ref[1 + i * tile : 1 + (i + 1) * tile, j * tile : (j + 1) * tile] = (
                own_tiles[i, j] * scale.astype(BF16)[None]
            )
        ready = (i + 1) * tile // 2 - (i < tr_dev - 1)
        for row in range(2 * done, 2 * ready, 2):
            z = dot(jnp.concatenate([x_ref[row + n] for n in range(4)], axis=1), w_ref[...])
            for ro in range(2):
                total = side_sums(z, 3 * ro * ch, nothing, nothing) + bias
                col_ref[0, row + ro : row + ro + 1] = total[0:1]
                col_ref[1, row + ro : row + ro + 1] = total[width - 1 : width]
                if row + ro == 0:
                    row_ref[0] = total
                if row + ro == height - 1:
                    row_ref[1] = total
                hid_ref[row + ro] = (gelu(total) * m_ref[row // tile]).astype(BF16)
            if (row + 2) % (tile // 2) == 0:
                stores.append(store(len(stores), row + 2 - tile // 2))
                stores[-1].start()
        done = ready
    for copy in stores:
        copy.wait()


def second_kernel(
    wet_ref, seam_ref, count_ref, fields_ref, made_ref, col_ref, row_ref, top_ref, bottom_ref,
    north_ref, south_ref, west_ref, east_ref, lcol_ref, rcol_ref, k1_ref, b1_ref, k2_ref, b2_ref, mix_ref, keep_ref, give_ref,
    own_tiles, out_ref, hid_ref, br_ref, w1_ref, w2_ref, mm_ref, pack_ref, own_ref, ext_ref, t_ref,
    zw1_ref, ze1_ref, zw2_ref, ze2_ref, hid_sem, in_sems, sems,
):
    tr_dev, tc_dev, tile, _, ch = fields_ref.shape
    width, height = tc_dev * tile, tr_dev * tile
    slots = keep_ref.shape[0]
    tall = 3 + (tile + 2) * tr_dev + 3
    lines = tall - 2
    loads = [
        pltpu.make_async_copy(fields_ref.at[i], own_tiles.at[i], in_sems.at[i]) for i in range(tr_dev)
    ]
    hid_load = pltpu.make_async_copy(made_ref, hid_ref.at[1 : height + 1], hid_sem)
    hid_load.start()
    for dy in range(3):
        for dx in range(3):
            w1_ref[dy * ch : (dy + 1) * ch, dx * ch : (dx + 1) * ch] = k1_ref[dy, dx]
    fill_weights(k2_ref, w2_ref)
    zero = jnp.zeros((ch, ch), BF16)
    mm_ref[:ch, :ch] = mix_ref[...]
    mm_ref[ch:, ch:] = mix_ref[...]
    mm_ref[:ch, ch:] = zero
    mm_ref[ch:, :ch] = zero
    bias1 = b1_ref[...]
    bias2 = b2_ref[...]
    rows = lax.broadcasted_iota(jnp.int32, (tile, tile), 0)
    cols = lax.broadcasted_iota(jnp.int32, (tile, tile), 1)
    flip = jnp.where(rows + cols == tile - 1, 1.0, 0.0).astype(BF16)

    notes = [ref[2 * width : 2 * width + 16].astype(F32) for ref in (north_ref, south_ref)]
    flagged = [[note[4 + tc_dev + s : 5 + tc_dev + s] > 0.5 for s in range(2)] for note in notes]

    step_size = height + 8
    sides = ((west_ref, lcol_ref.at[0], 0), (east_ref, rcol_ref.at[1], width - 1))
    for s, (pack, own, c) in enumerate(sides):
        pack_ref[s] = pack[...].astype(F32)
        own_ref[s, 1 : height + 1] = own[...].astype(F32)
        own_ref[s, 0:1] = pixel(north_ref, width + c)
        own_ref[s, height + 1 : height + 2] = pixel(south_ref, c)
    for s, (pack, own, c) in enumerate(sides):
        near = step_size * (1 - s)
        far = step_size * s
        notes_at = 2 * step_size
        note = [pack_ref[s, notes_at + n : notes_at + n + 1] for n in range(8)]
        held = pack_ref.at[s]
        mine = own_ref.at[s]
        flags = [seam_line(seam_ref, i, s * (tc_dev - 1), s, ch) for i in range(tr_dev)]
        north_flag, south_flag = flagged[0][s], flagged[1][s]

        def near_line(n, near=near, held=held):
            return held[near + n : near + n + 1]

        above = [
            jnp.where(north_flag, note[1], near_line(0)),
            jnp.where(north_flag, note[0], near_line(1)),
            near_line(2),
        ]
        below = [
            near_line(height + 1),
            jnp.where(south_flag, note[3], near_line(height + 2)),
            jnp.where(south_flag, note[2], near_line(height + 3)),
        ]
        put_pads(t_ref.at[0], above, held, near + 1, flags, below, flip, tile)
        z_ref = (zw1_ref, ze1_ref)[s]
        z_ref[0:lines] = tall_conv(t_ref.at[0], k1_ref, 2 * s, lines)
        total = bias1
        put_columns(t_ref.at[1], held, near, tr_dev, tile)
        total = total + tall_conv(t_ref.at[1], k1_ref, 1, lines)
        put_columns(t_ref.at[2], held, far, tr_dev, tile)
        total = total + tall_conv(t_ref.at[2], k1_ref, 2 * s, lines)
        above = [
            jnp.where(north_flag, notes[0][2 * s + 1 : 2 * s + 2], pixel(north_ref, c)),
            jnp.where(north_flag, notes[0][2 * s : 2 * s + 1], pixel(north_ref, width + c)),
            mine[1:2],
        ]
        below = [
            mine[height : height + 1],
            jnp.where(south_flag, notes[1][2 * s + 1 : 2 * s + 2], pixel(south_ref, c)),
            jnp.where(south_flag, notes[1][2 * s : 2 * s + 1], pixel(south_ref, width + c)),
        ]
        put_pads(t_ref.at[3], above, mine, 0, flags, below, flip, tile)
        total = total + tall_conv(t_ref.at[3], k1_ref, 2 - 2 * s, lines)
        value = gelu(total)
        spare = ext_ref.at[s]
        spare[0:1] = value[0:1] * note[4 + tr_dev]
        for i in range(tr_dev):
            at = line_at(i * tile, tile)
            spare[1 + i * tile : 1 + (i + 1) * tile] = value[at : at + tile] * note[4 + i]
        spare[height + 1 : height + 2] = value[lines - 1 : lines] * note[5 + tr_dev]
        put_pads(t_ref.at[0], [], spare, 0, flags, [], flip, tile)
        z_ref = (zw2_ref, ze2_ref)[s]
        z_ref[0:lines] = tall_conv(t_ref.at[0], k2_ref, 2 * s, lines)

    beyond = (
        (0, [north_ref[0:width], north_ref[width : 2 * width], top_ref[0:width]], 0, notes[0]),
        (
            height + 1,
            [bottom_ref[width : 2 * width], south_ref[0:width], south_ref[width : 2 * width]],
            lines - 1,
            notes[1],
        ),
    )
    for row, window, line, note in beyond:
        z = dot(jnp.concatenate(window, axis=1), w1_ref[...])
        total = side_sums(z, 0, zw1_ref[line : line + 1], ze1_ref[line : line + 1]) + bias1
        value = gelu(total)
        for j in range(tc_dev):
            hid_ref[row, j * tile : (j + 1) * tile] = (
                value[j * tile : (j + 1) * tile] * note[4 + j : 5 + j]
            ).astype(BF16)

    hid_load.wait()
    for load in loads:
        load.start()
    part = 16
    for s in range(2):
        z_ref = (zw1_ref, ze1_ref)[s]
        at = s * (width - part)
        place_in = lax.broadcasted_iota(jnp.int32, (tile, part, ch), 1)
        for i in range(tr_dev):
            line = line_at(i * tile, tile)
            total = col_ref[s, i * tile : (i + 1) * tile] + z_ref[line : line + tile]
            value = gelu(total) * wet_ref[i, s * (tc_dev - 1)].astype(F32)
            held = hid_ref[1 + i * tile : 1 + (i + 1) * tile, at : at + part].astype(F32)
            fixed = jnp.where(place_in == s * (part - 1), value[:, None, :], held)
            hid_ref[1 + i * tile : 1 + (i + 1) * tile, at : at + part] = fixed.astype(BF16)
    for n, outer in enumerate((north_ref[width : 2 * width], south_ref[0:width])):
        row = n * (height - 1)
        line = line_at(row, tile)
        z = dot(outer, w1_ref[2 * n * ch : (2 * n + 1) * ch])
        total = row_ref[n] + side_sums(z, 0, zw1_ref[line : line + 1], ze1_ref[line : line + 1])
        value = gelu(total)
        for j in range(tc_dev):
            wet = wet_ref[row // tile, j].astype(F32)
            hid_ref[1 + row, j * tile : (j + 1) * tile] = (
                value[j * tile : (j + 1) * tile] * wet
            ).astype(BF16)

    def branch(p):
        row = 2 * p
        window = [hid_ref[row + k] for k in range(4)]
        outs = conv_pair(window, w2_ref, bias2, zw2_ref, ze2_ref, line_at(row, tile))
        for ro in range(2):
            br_ref[p, :, ro * ch : (ro + 1) * ch] = gelu(outs[ro]).astype(BF16)

    def mix(p):
        i = 2 * p // tile
        inner = 2 * p % tile
        mixed = dot(br_ref[p], mm_ref[...])
        for ro in range(2):
            own = own_tiles[i, :, inner + ro].reshape(width, ch).astype(F32)
            total = (own + mixed[:, ro * ch : (ro + 1) * ch]).astype(BF16)
            out_ref[i, :, inner + ro] = total.reshape(tc_dev, tile, ch)

    def second(p, carry):
        branch(p)
        return carry

    def third(p, carry):
        mix(p)
        return carry

    place = lax.axis_index("col")
    rank = wet_before(count_ref, place)
    odd = place % 2
    targets = []
    given = 0
    for i in range(tr_dev):
        for j in range(tc_dev):
            kept = rank % 2 == odd
            slot = jnp.where(kept, rank % (2 * slots) // 2, slots + given // 2)
            targets.append(jnp.where(wet_ref[i, j] == 1, slot, -1))
            rank += wet_ref[i, j]
            given += wet_ref[i, j]

    def start_copies(i):
        for j in range(tc_dev):
            k = i * tc_dev + j
            target = targets[k]

            @pl.when((target >= 0) & (target < slots))
            def _():
                pltpu.make_async_copy(out_ref.at[i, j], keep_ref.at[target], sems.at[k]).start()

            @pl.when(target >= slots)
            def _():
                pltpu.make_async_copy(
                    out_ref.at[i, j], give_ref.at[target - slots], sems.at[k]
                ).start()

    def wait_copies(i):
        for j in range(tc_dev):
            k = i * tc_dev + j

            @pl.when(wet_ref[i, j] == 1)
            def _():
                pltpu.make_async_copy(out_ref.at[i, j], keep_ref.at[0], sems.at[k]).wait()

    for i in range(tr_dev):
        lax.fori_loop(i * tile // 2, (i + 1) * tile // 2, second, 0, unroll=tile // 2)
        loads[i].wait()
        lax.fori_loop(i * tile // 2, (i + 1) * tile // 2, third, 0, unroll=8)
        start_copies(i)
    for i in range(tr_dev):
        wait_copies(i)


def scatter_kernel(count_ref, src_ref, held_ref, out_ref, sems):
    slots = out_ref.shape[0]
    place = lax.axis_index("col")
    odd = place % 2
    mate = place + 1 - 2 * odd
    start = wet_before(count_ref, mate)
    stop = wet_before(count_ref, mate + 1)
    ranks = [start + 2 * k + (start + odd) % 2 for k in range(src_ref.shape[0])]

    def each(act):
        for k, rank in enumerate(ranks):

            @pl.when(rank < stop)
            def _():
                act(k)

    def store(k):
        slot = ranks[k] % (2 * slots) // 2
        return pltpu.make_async_copy(src_ref.at[k], out_ref.at[slot], sems.at[k])

    each(lambda k: store(k).start())
    each(lambda k: store(k).wait())


def gather_kernel(across, list_ref, src_ref, out_ref, sems):
    chips = src_ref.shape[0]
    copies = []
    for k in range(out_ref.shape[0]):
        chip = list_ref[k] % across // (across // chips)
        copies.append(pltpu.make_async_copy(src_ref.at[chip], out_ref.at[k], sems.at[k]))
    for copy in copies:
        copy.start()
    for copy in copies:
        copy.wait()


def shifted(x, axis, step):
    count = lax.axis_size(axis)
    pairs = [(i, i + step) for i in range(count) if 0 <= i + step < count]
    return lax.ppermute(x, axis, pairs)


def on_device(
    fields, wet_mask, seam_flags, wet_list, kernel_one, bias_one, kernel_two, bias_two, mixing
):
    tr_dev, tc_dev, tile, _, ch = fields.shape
    face = tr_dev * tc_dev
    wet_dev = wet_list.shape[0]
    columns = lax.axis_size("col")
    chips = columns // 2
    width, height = tc_dev * tile, tr_dev * tile
    half = face // 2
    seams = pltpu.with_memory_space_constraint(jnp.swapaxes(seam_flags, 1, 2), pltpu.HBM)
    wet_mask = pltpu.with_memory_space_constraint(wet_mask, pltpu.HBM)
    params = pltpu.CompilerParams(vmem_limit_bytes=VMEM_LIMIT)
    small = pltpu.CompilerParams(vmem_limit_bytes=VMEM_LIMIT // 6)
    fields = pltpu.with_memory_space_constraint(fields, pltpu.HBM)
    strip = jax.ShapeDtypeStruct((2 * width + 16, ch), BF16)
    pair = jax.ShapeDtypeStruct((2, height, ch), BF16)
    top, bottom, lcols, rcols, count = pl.pallas_call(
        rim_kernel,
        out_shape=(strip, strip, pair, pair, jax.ShapeDtypeStruct((columns, 1, ch), F32)),
        in_specs=[SCALARS, SCALARS, IN_HBM],
        out_specs=(WHOLE,) * 5,
        scratch_shapes=[
            pltpu.VMEM((2, tc_dev, 2, tile, ch), BF16),
            pltpu.VMEM((2, tr_dev, tile, 16, ch), BF16),
            pltpu.VMEM((2, height * 16, ch), F32),
            pltpu.SemaphoreType.DMA((4,)),
        ],
        compiler_params=small,
        name="rim",
    )(wet_mask, seams, fields)
    north = shifted(bottom, "row", 1)
    south = shifted(top, "row", -1)
    counts = lax.all_to_all(count, "col", split_axis=0, concat_axis=0, tiled=True)
    pack = jax.ShapeDtypeStruct((2 * (height + 8) + 16, ch), BF16)
    left, right = pl.pallas_call(
        side_kernel,
        out_shape=(pack, pack),
        in_specs=[SCALARS] + [WHOLE] * 4,
        out_specs=(WHOLE,) * 2,
        scratch_shapes=[pltpu.VMEM(pack.shape, F32)],
        compiler_params=small,
        name="side",
    )(wet_mask, north, south, lcols, rcols)

    tile_shape = (tile, tile, ch)
    lines = 8 + (tile + 2) * tr_dev
    lines += -lines % 8
    hid, edge_cols, edge_rows = pl.pallas_call(
        first_kernel,
        out_shape=(
            pltpu.HBM((height, width, ch), BF16),
            jax.ShapeDtypeStruct((2, height, ch), F32),
            jax.ShapeDtypeStruct((2, width, ch), F32),
        ),
        in_specs=[SCALARS, IN_HBM, WHOLE, WHOLE],
        out_specs=(IN_HBM, WHOLE, WHOLE),
        scratch_shapes=[
            pltpu.VMEM(fields.shape, BF16),
            pltpu.VMEM((height + 2, width, ch), BF16),
            pltpu.VMEM((height, width, ch), BF16),
            pltpu.VMEM((4 * ch, 6 * ch), BF16),
            pltpu.VMEM((tr_dev, width, ch), F32),
            pltpu.SemaphoreType.DMA((tr_dev,)),
            pltpu.SemaphoreType.DMA((2 * tr_dev,)),
        ],
        compiler_params=params,
        name="first_conv",
    )(wet_mask, fields, kernel_one, bias_one[None])

    hid = pltpu.with_memory_space_constraint(hid, pltpu.HBM)
    left, right, counts, edge_rows = lax.optimization_barrier((left, right, counts, edge_rows))
    west = shifted(right, "col", 1)
    east = shifted(left, "col", -1)
    keep, give = pl.pallas_call(
        second_kernel,
        out_shape=(
            jax.ShapeDtypeStruct((chips,) + tile_shape, BF16),
            jax.ShapeDtypeStruct((half,) + tile_shape, BF16),
        ),
        in_specs=[SCALARS, SCALARS, WHOLE, IN_HBM, IN_HBM] + [WHOLE] * 15,
        out_specs=(IN_PLACE, IN_PLACE),
        scratch_shapes=[
            pltpu.VMEM(fields.shape, BF16),
            pltpu.VMEM(fields.shape, BF16),
            pltpu.VMEM((height + 2, width, ch), BF16),
            pltpu.VMEM((height // 2, width, 2 * ch), BF16),
            pltpu.VMEM((3 * ch, 3 * ch), BF16),
            pltpu.VMEM((4 * ch, 6 * ch), BF16),
            pltpu.VMEM((2 * ch, 2 * ch), BF16),
            pltpu.VMEM((2,) + west.shape, F32),
            pltpu.VMEM((2, height + 8, ch), F32),
            pltpu.VMEM((2, height + 8, ch), F32),
            pltpu.VMEM((4, lines, ch), F32),
            pltpu.VMEM((lines, ch), F32),
            pltpu.VMEM((lines, ch), F32),
            pltpu.VMEM((lines, ch), F32),
            pltpu.VMEM((lines, ch), F32),
            pltpu.SemaphoreType.DMA,
            pltpu.SemaphoreType.DMA((tr_dev,)),
            pltpu.SemaphoreType.DMA((face,)),
        ],
        compiler_params=params,
        name="second_conv",
    )(
        wet_mask, seams, counts, fields, hid, edge_cols, edge_rows, top, bottom,
        north, south, west, east, lcols, rcols,
        kernel_one, bias_one[None], kernel_two, bias_two[None], mixing,
    )

    taken = lax.ppermute(give, "col", [(i, i ^ 1) for i in range(columns)])
    sending = pl.pallas_call(
        scatter_kernel,
        out_shape=jax.ShapeDtypeStruct(keep.shape, BF16),
        in_specs=[WHOLE, WHOLE, IN_PLACE],
        out_specs=IN_PLACE,
        scratch_shapes=[pltpu.SemaphoreType.DMA((half,))],
        input_output_aliases={2: 0},
        compiler_params=small,
        name="merge_mate",
    )(counts, taken, keep)
    groups = [[2 * k + c for k in range(chips)] for c in range(2)]
    arrived = lax.all_to_all(
        sending, "col", split_axis=0, concat_axis=0, tiled=True, axis_index_groups=groups
    )
    return pl.pallas_call(
        functools.partial(gather_kernel, tc_dev * columns),
        out_shape=jax.ShapeDtypeStruct((wet_dev,) + tile_shape, BF16),
        in_specs=[SCALARS, WHOLE],
        out_specs=IN_HBM,
        scratch_shapes=[pltpu.SemaphoreType.DMA((wet_dev,))],
        compiler_params=small,
        name="slot_order",
    )(wet_list, arrived)


def solution(mesh):
    return jax.shard_map(
        on_device,
        mesh=mesh,
        in_specs=(
            P("row", "col", None, None, None),
            P("row", "col"),
            P("row", "col", None),
            P(("row", "col")),
            P(),
            P(),
            P(),
            P(),
            P(),
        ),
        out_specs=P(("row", "col"), None, None, None),
        check_vma=False,
    )
```

```python
import functools

import jax
import jax.numpy as jnp
from jax import lax
from jax.experimental import pallas as pl
from jax.experimental.pallas import tpu as pltpu
from jax.sharding import PartitionSpec as P

F32 = jnp.float32
BF16 = jnp.bfloat16
VMEM_LIMIT = 32 * 1024 * 1024
WHOLE = pl.BlockSpec(memory_space=pltpu.VMEM)
SCALARS = pl.BlockSpec(memory_space=pltpu.SMEM)
IN_PLACE = pl.BlockSpec(memory_space=pl.ANY)
IN_HBM = pl.BlockSpec(memory_space=pltpu.HBM)


def dot(a, b):
    return jnp.dot(a, b, preferred_element_type=F32)


def gelu(x):
    u = x * (0.7978845608028654 + 0.03567740813636141 * (x * x))
    half = 0.5 * x
    return half + half * jnp.tanh(u)


def fill_weights(k_ref, w_ref):
    ch = k_ref.shape[2]
    zero = jnp.zeros((ch, 3 * ch), BF16)
    w_ref[3 * ch :, : 3 * ch] = zero
    w_ref[:ch, 3 * ch :] = zero
    for dy in range(3):
        for dx in range(3):
            block = k_ref[dy, dx]
            w_ref[dy * ch : (dy + 1) * ch, dx * ch : (dx + 1) * ch] = block
            w_ref[(dy + 1) * ch : (dy + 2) * ch, (3 + dx) * ch : (4 + dx) * ch] = block


def tall_conv(t_ref, k_ref, dx, count):
    total = dot(t_ref[0:count].astype(BF16), k_ref[0, dx])
    total += dot(t_ref[1 : count + 1].astype(BF16), k_ref[1, dx])
    total += dot(t_ref[2 : count + 2].astype(BF16), k_ref[2, dx])
    return total


def put_columns(t_ref, col_ref, base, tr_dev, tile):
    tall = tile + 2
    t_ref[0:3] = col_ref[base : base + 3]
    for i in range(tr_dev):
        t_ref[3 + tall * i : 3 + tall * (i + 1)] = col_ref[
            base + 1 + tile * i : base + 1 + tile * i + tall
        ]
    last = 3 + tall * tr_dev
    t_ref[last : last + 3] = col_ref[base + 1 + tile * tr_dev : base + 4 + tile * tr_dev]


def put_pads(t_ref, above, ext_ref, base, flags, below, flip, tile):
    tall = tile + 2
    for n, line in enumerate(above):
        t_ref[n : n + 1] = line
    for i, flag in enumerate(flags):
        at = 3 + tall * i
        from_row = base + tile * i
        t_ref[at : at + 1] = ext_ref[from_row : from_row + 1]
        middle = ext_ref[from_row + 1 : from_row + 1 + tile]
        turned = dot(flip, middle.astype(BF16))
        t_ref[at + 1 : at + 1 + tile] = jnp.where(flag > 0.5, turned, middle)
        t_ref[at + tall - 1 : at + tall] = ext_ref[from_row + tile + 1 : from_row + tile + 2]
    last = 3 + tall * len(flags)
    for n, line in enumerate(below):
        t_ref[last + n : last + n + 1] = line


def line_at(tall_row, tile):
    return 3 + tall_row + 2 * (tall_row // tile)


def side_sums(z, taps, west, east):
    ch = west.shape[1]
    width = z.shape[0]
    lane_row = lax.broadcasted_iota(jnp.int32, (8, ch), 0)
    left = pltpu.roll(z[:, taps : taps + ch], 1, 0)
    right = pltpu.roll(z[:, taps + 2 * ch : taps + 3 * ch], width - 1, 0)
    left = jnp.concatenate([jnp.where(lane_row == 0, west, left[:8]), left[8:]], axis=0)
    right = jnp.concatenate(
        [right[: width - 8], jnp.where(lane_row == 7, east, right[width - 8 :])], axis=0
    )
    return z[:, taps + ch : taps + 2 * ch] + left + right


def conv_pair(window, w_ref, bias, zw_ref, ze_ref, line):
    ch = window[0].shape[1]
    z = dot(jnp.concatenate(window, axis=1), w_ref[...])
    outs = []
    for ro in range(2):
        west = zw_ref[pl.ds(line + ro, 1), :]
        east = ze_ref[pl.ds(line + ro, 1), :]
        outs.append(side_sums(z, 3 * ro * ch, west, east) + bias)
    return outs


def seam_line(seam_ref, i, j, side, ch):
    return jnp.full((1, ch), 1.0, F32) * seam_ref[i, side, j].astype(F32)


def rim_kernel(
    wet_ref, seam_ref, fields_ref, top_ref, bottom_ref, lcol_ref, rcol_ref, count_ref,
    rows_ref, cols_ref, line_ref, sems,
):
    tr_dev, tc_dev, tile, _, ch = fields_ref.shape
    width, height = tc_dev * tile, tr_dev * tile
    part = cols_ref.shape[3]
    loads = [
        pltpu.make_async_copy(fields_ref.at[0, :, 0:2], rows_ref.at[0], sems.at[0]),
        pltpu.make_async_copy(fields_ref.at[tr_dev - 1, :, tile - 2 : tile], rows_ref.at[1], sems.at[1]),
        pltpu.make_async_copy(fields_ref.at[:, 0, :, 0:part], cols_ref.at[0], sems.at[2]),
        pltpu.make_async_copy(fields_ref.at[:, tc_dev - 1, :, tile - part :], cols_ref.at[1], sems.at[3]),
    ]
    for load in loads:
        load.start()

    def wet(i, j):
        return jnp.full((1, ch), 1.0, F32) * wet_ref[i, j].astype(F32)

    total = sum(wet_ref[i, j] for i in range(tr_dev) for j in range(tc_dev))
    count_ref[...] = jnp.full(count_ref.shape, 1.0, F32) * total.astype(F32)
    for load in loads:
        load.wait()
    for side, (out_ref, i) in enumerate(((top_ref, 0), (bottom_ref, tr_dev - 1))):
        for j in range(tc_dev):
            scale = wet(i, j).astype(BF16)
            for n in range(2):
                out_ref[n * width + j * tile : n * width + (j + 1) * tile] = (
                    rows_ref[side, j, n] * scale
                )
    picked = []
    for side, out_ref in enumerate((lcol_ref, rcol_ref)):
        for i in range(tr_dev):
            block = cols_ref[side, i].astype(F32) * wet(i, side * (tc_dev - 1))[None]
            line_ref[side, i * tile * part : (i + 1) * tile * part] = block.reshape(tile * part, ch)
        first = side * (part - 2)
        columns = [line_ref[side, pl.ds(first + n, height, stride=part)] for n in range(2)]
        out_ref[0] = columns[0].astype(BF16)
        out_ref[1] = columns[1].astype(BF16)
        picked.append(columns[side])
    for out_ref, i, near in ((top_ref, 0, tile - 2), (bottom_ref, tr_dev - 1, tile * (tr_dev - 1))):
        extra = [column[near : near + 2] for column in picked]
        extra += [wet(i, j) for j in range(tc_dev)]
        extra += [
            seam_line(seam_ref, i, side * (tc_dev - 1), side, ch) for side in range(2)
        ]
        extra.append(jnp.zeros((12 - tc_dev - 2, ch), F32))
        at = 0
        for piece in extra:
            line_ref[0, at : at + piece.shape[0]] = piece
            at += piece.shape[0]
        out_ref[2 * width : 2 * width + 16] = line_ref[0, 0:16].astype(BF16)


def pixel(ref, n):
    base = n // 16 * 16
    return ref[base : base + 16].astype(F32)[n - base : n - base + 1]


def side_kernel(wet_ref, north_ref, south_ref, lcol_ref, rcol_ref, left_ref, right_ref, line_ref):
    tr_dev, tc_dev = wet_ref.shape
    ch = north_ref.shape[1]
    height = lcol_ref.shape[1]
    width = (north_ref.shape[0] - 16) // 2
    span = height + 8
    notes = [ref[2 * width : 2 * width + 16].astype(F32) for ref in (north_ref, south_ref)]
    for s, (out_ref, own) in enumerate(((left_ref, lcol_ref), (right_ref, rcol_ref))):
        for n in range(2):
            c = s * (width - 2) + n
            at = n * span
            line_ref[at : at + 1] = pixel(north_ref, c)
            line_ref[at + 1 : at + 2] = pixel(north_ref, width + c)
            line_ref[at + 2 : at + 2 + height] = own[n].astype(F32)
            line_ref[at + 2 + height : at + 3 + height] = pixel(south_ref, c)
            line_ref[at + 3 + height : at + 4 + height] = pixel(south_ref, width + c)
            line_ref[at + 4 + height : at + span] = jnp.zeros((4, ch), F32)
        at = 2 * span
        j = s * (tc_dev - 1)
        line_ref[at : at + 16] = jnp.zeros((16, ch), F32)
        line_ref[at : at + 2] = notes[0][2 * s : 2 * s + 2]
        line_ref[at + 2 : at + 4] = notes[1][2 * s : 2 * s + 2]
        for i in range(tr_dev):
            line_ref[at + 4 + i : at + 5 + i] = jnp.full((1, ch), 1.0, F32) * wet_ref[i, j].astype(F32)
        line_ref[at + 4 + tr_dev : at + 5 + tr_dev] = notes[0][4 + j : 5 + j]
        line_ref[at + 5 + tr_dev : at + 6 + tr_dev] = notes[1][4 + j : 5 + j]
        out_ref[...] = line_ref[...].astype(BF16)


def wet_before(count_ref, place):
    row = lax.broadcasted_iota(jnp.int32, count_ref.shape, 0)
    earlier = jnp.where(row < place, count_ref[...], 0.0)
    return jnp.max(jnp.sum(earlier, axis=0)).astype(jnp.int32)


def conv_kernel(
    wet_ref, seam_ref, count_ref, fields_ref, north_ref, south_ref, west_ref, east_ref,
    lcol_ref, rcol_ref, k1_ref, b1_ref, k2_ref, b2_ref, mix_ref, keep_ref, give_ref,
    own_tiles, out_ref, x_ref, hid_ref, br_ref, w1_ref, w2_ref, mm_ref, m_ref, pack_ref, own_ref, ext_ref, t_ref,
    zw1_ref, ze1_ref, zw2_ref, ze2_ref, in_sems, sems,
):
    tr_dev, tc_dev, tile, _, ch = fields_ref.shape
    width, height = tc_dev * tile, tr_dev * tile
    slots = keep_ref.shape[0]
    tall = 3 + (tile + 2) * tr_dev + 3
    lines = tall - 2
    loads = [
        pltpu.make_async_copy(fields_ref.at[i], own_tiles.at[i], in_sems.at[i]) for i in range(tr_dev)
    ]
    for load in loads:
        load.start()
    fill_weights(k1_ref, w1_ref)
    fill_weights(k2_ref, w2_ref)
    zero = jnp.zeros((ch, ch), BF16)
    mm_ref[:ch, :ch] = mix_ref[...]
    mm_ref[ch:, ch:] = mix_ref[...]
    mm_ref[:ch, ch:] = zero
    mm_ref[ch:, :ch] = zero
    bias1 = b1_ref[...]
    bias2 = b2_ref[...]
    rows = lax.broadcasted_iota(jnp.int32, (tile, tile), 0)
    cols = lax.broadcasted_iota(jnp.int32, (tile, tile), 1)
    flip = jnp.where(rows + cols == tile - 1, 1.0, 0.0).astype(BF16)

    notes = [ref[2 * width : 2 * width + 16].astype(F32) for ref in (north_ref, south_ref)]
    flagged = [[note[4 + tc_dev + s : 5 + tc_dev + s] > 0.5 for s in range(2)] for note in notes]

    step_size = height + 8
    sides = ((west_ref, lcol_ref.at[0], 0), (east_ref, rcol_ref.at[1], width - 1))
    for s, (pack, own, c) in enumerate(sides):
        pack_ref[s] = pack[...].astype(F32)
        own_ref[s, 1 : height + 1] = own[...].astype(F32)
        own_ref[s, 0:1] = pixel(north_ref, width + c)
        own_ref[s, height + 1 : height + 2] = pixel(south_ref, c)
    for s, (pack, own, c) in enumerate(sides):
        near = step_size * (1 - s)
        far = step_size * s
        notes_at = 2 * step_size
        note = [pack_ref[s, notes_at + n : notes_at + n + 1] for n in range(8)]
        held = pack_ref.at[s]
        mine = own_ref.at[s]
        flags = [seam_line(seam_ref, i, s * (tc_dev - 1), s, ch) for i in range(tr_dev)]
        north_flag, south_flag = flagged[0][s], flagged[1][s]

        def near_line(n, near=near, held=held):
            return held[near + n : near + n + 1]

        above = [
            jnp.where(north_flag, note[1], near_line(0)),
            jnp.where(north_flag, note[0], near_line(1)),
            near_line(2),
        ]
        below = [
            near_line(height + 1),
            jnp.where(south_flag, note[3], near_line(height + 2)),
            jnp.where(south_flag, note[2], near_line(height + 3)),
        ]
        put_pads(t_ref.at[0], above, held, near + 1, flags, below, flip, tile)
        z_ref = (zw1_ref, ze1_ref)[s]
        z_ref[0:lines] = tall_conv(t_ref.at[0], k1_ref, 2 * s, lines)
        total = bias1
        put_columns(t_ref.at[1], held, near, tr_dev, tile)
        total = total + tall_conv(t_ref.at[1], k1_ref, 1, lines)
        put_columns(t_ref.at[2], held, far, tr_dev, tile)
        total = total + tall_conv(t_ref.at[2], k1_ref, 2 * s, lines)
        above = [
            jnp.where(north_flag, notes[0][2 * s + 1 : 2 * s + 2], pixel(north_ref, c)),
            jnp.where(north_flag, notes[0][2 * s : 2 * s + 1], pixel(north_ref, width + c)),
            mine[1:2],
        ]
        below = [
            mine[height : height + 1],
            jnp.where(south_flag, notes[1][2 * s + 1 : 2 * s + 2], pixel(south_ref, c)),
            jnp.where(south_flag, notes[1][2 * s : 2 * s + 1], pixel(south_ref, width + c)),
        ]
        put_pads(t_ref.at[3], above, mine, 0, flags, below, flip, tile)
        total = total + tall_conv(t_ref.at[3], k1_ref, 2 - 2 * s, lines)
        value = gelu(total)
        spare = ext_ref.at[s]
        spare[0:1] = value[0:1] * note[4 + tr_dev]
        for i in range(tr_dev):
            at = line_at(i * tile, tile)
            spare[1 + i * tile : 1 + (i + 1) * tile] = value[at : at + tile] * note[4 + i]
        spare[height + 1 : height + 2] = value[lines - 1 : lines] * note[5 + tr_dev]
        put_pads(t_ref.at[0], [], spare, 0, flags, [], flip, tile)
        z_ref = (zw2_ref, ze2_ref)[s]
        z_ref[0:lines] = tall_conv(t_ref.at[0], k2_ref, 2 * s, lines)

    x_ref[0] = north_ref[width : 2 * width]
    x_ref[height + 1] = south_ref[0:width]

    def fill(i):
        loads[i].wait()
        for j in range(tc_dev):
            scale = jnp.full((1, ch), 1.0, F32) * wet_ref[i, j].astype(F32)
            m_ref[i, j * tile : (j + 1) * tile] = jnp.broadcast_to(scale, (tile, ch))
            x_ref[1 + i * tile : 1 + (i + 1) * tile, j * tile : (j + 1) * tile] = (
                own_tiles[i, j] * scale.astype(BF16)[None]
            )

    beyond = (
        (0, [north_ref.at[0:width], north_ref.at[width : 2 * width], x_ref.at[1]], 0, notes[0]),
        (height + 1, [x_ref.at[height], south_ref.at[0:width], south_ref.at[width : 2 * width]], lines - 1, notes[1]),
    )

    def outside(row, window, line, note):
        window = [w[...] for w in window]
        z = dot(jnp.concatenate(window, axis=1), w1_ref[: 3 * ch, : 3 * ch])
        total = side_sums(z, 0, zw1_ref[line : line + 1], ze1_ref[line : line + 1]) + bias1
        value = gelu(total)
        for j in range(tc_dev):
            hid_ref[row, j * tile : (j + 1) * tile] = (
                value[j * tile : (j + 1) * tile] * note[4 + j : 5 + j]
            ).astype(BF16)

    def first(p, carry):
        row = 2 * p
        window = [x_ref[row + k] for k in range(4)]
        outs = conv_pair(window, w1_ref, bias1, zw1_ref, ze1_ref, line_at(row, tile))
        for ro in range(2):
            hid_ref[1 + row + ro] = (gelu(outs[ro]) * m_ref[row // tile]).astype(BF16)
        return carry

    def branch(p):
        row = 2 * p
        window = [hid_ref[row + k] for k in range(4)]
        outs = conv_pair(window, w2_ref, bias2, zw2_ref, ze2_ref, line_at(row, tile))
        for ro in range(2):
            br_ref[p, :, ro * ch : (ro + 1) * ch] = gelu(outs[ro]).astype(BF16)

    def mix(p):
        i = 2 * p // tile
        inner = 2 * p % tile
        mixed = dot(br_ref[p], mm_ref[...])
        for ro in range(2):
            own = own_tiles[i, :, inner + ro].reshape(width, ch).astype(F32)
            total = (own + mixed[:, ro * ch : (ro + 1) * ch]).astype(BF16)
            out_ref[i, :, inner + ro] = total.reshape(tc_dev, tile, ch)

    def second(p, carry):
        branch(p)
        return carry

    def third(p, carry):
        mix(p)
        return carry

    place = lax.axis_index("col")
    rank = wet_before(count_ref, place)
    odd = place % 2
    targets = []
    given = 0
    for i in range(tr_dev):
        for j in range(tc_dev):
            kept = rank % 2 == odd
            slot = jnp.where(kept, rank % (2 * slots) // 2, slots + given // 2)
            targets.append(jnp.where(wet_ref[i, j] == 1, slot, -1))
            rank += wet_ref[i, j]
            given += wet_ref[i, j]

    def start_copies(i):
        for j in range(tc_dev):
            k = i * tc_dev + j
            target = targets[k]

            @pl.when((target >= 0) & (target < slots))
            def _():
                pltpu.make_async_copy(out_ref.at[i, j], keep_ref.at[target], sems.at[k]).start()

            @pl.when(target >= slots)
            def _():
                pltpu.make_async_copy(
                    out_ref.at[i, j], give_ref.at[target - slots], sems.at[k]
                ).start()

    def wait_copies(i):
        for j in range(tc_dev):
            k = i * tc_dev + j

            @pl.when(wet_ref[i, j] == 1)
            def _():
                pltpu.make_async_copy(out_ref.at[i, j], keep_ref.at[0], sems.at[k]).wait()

    done = 0
    for i in range(tr_dev):
        fill(i)
        if i == 0:
            outside(*beyond[0])
        if i == tr_dev - 1:
            outside(*beyond[1])
        ready = (i + 1) * tile // 2 - (i < tr_dev - 1)
        lax.fori_loop(done, ready, first, 0, unroll=ready - done)
        done = ready
    for i in range(tr_dev):
        lax.fori_loop(i * tile // 2, (i + 1) * tile // 2, second, 0, unroll=tile // 2)
        lax.fori_loop(i * tile // 2, (i + 1) * tile // 2, third, 0, unroll=8)
        start_copies(i)
    for i in range(tr_dev):
        wait_copies(i)


def scatter_kernel(count_ref, src_ref, held_ref, out_ref, sems):
    slots = out_ref.shape[0]
    place = lax.axis_index("col")
    odd = place % 2
    mate = place + 1 - 2 * odd
    start = wet_before(count_ref, mate)
    stop = wet_before(count_ref, mate + 1)
    ranks = [start + 2 * k + (start + odd) % 2 for k in range(src_ref.shape[0])]

    def each(act):
        for k, rank in enumerate(ranks):

            @pl.when(rank < stop)
            def _():
                act(k)

    def store(k):
        slot = ranks[k] % (2 * slots) // 2
        return pltpu.make_async_copy(src_ref.at[k], out_ref.at[slot], sems.at[k])

    each(lambda k: store(k).start())
    each(lambda k: store(k).wait())


def gather_kernel(across, list_ref, src_ref, out_ref, sems):
    chips = src_ref.shape[0]
    copies = []
    for k in range(out_ref.shape[0]):
        chip = list_ref[k] % across // (across // chips)
        copies.append(pltpu.make_async_copy(src_ref.at[chip], out_ref.at[k], sems.at[k]))
    for copy in copies:
        copy.start()
    for copy in copies:
        copy.wait()


def shifted(x, axis, step):
    count = lax.axis_size(axis)
    pairs = [(i, i + step) for i in range(count) if 0 <= i + step < count]
    return lax.ppermute(x, axis, pairs)


def on_device(
    fields, wet_mask, seam_flags, wet_list, kernel_one, bias_one, kernel_two, bias_two, mixing
):
    tr_dev, tc_dev, tile, _, ch = fields.shape
    face = tr_dev * tc_dev
    wet_dev = wet_list.shape[0]
    columns = lax.axis_size("col")
    chips = columns // 2
    width, height = tc_dev * tile, tr_dev * tile
    half = face // 2
    seams = pltpu.with_memory_space_constraint(jnp.swapaxes(seam_flags, 1, 2), pltpu.HBM)
    wet_mask = pltpu.with_memory_space_constraint(wet_mask, pltpu.HBM)
    params = pltpu.CompilerParams(vmem_limit_bytes=VMEM_LIMIT)
    small = pltpu.CompilerParams(vmem_limit_bytes=VMEM_LIMIT // 8)
    fields = pltpu.with_memory_space_constraint(fields, pltpu.HBM)
    strip = jax.ShapeDtypeStruct((2 * width + 16, ch), BF16)
    pair = jax.ShapeDtypeStruct((2, height, ch), BF16)
    top, bottom, lcols, rcols, count = pl.pallas_call(
        rim_kernel,
        out_shape=(strip, strip, pair, pair, jax.ShapeDtypeStruct((columns, 1, ch), F32)),
        in_specs=[SCALARS, SCALARS, IN_HBM],
        out_specs=(WHOLE,) * 5,
        scratch_shapes=[
            pltpu.VMEM((2, tc_dev, 2, tile, ch), BF16),
            pltpu.VMEM((2, tr_dev, tile, 16, ch), BF16),
            pltpu.VMEM((2, height * 16, ch), F32),
            pltpu.SemaphoreType.DMA((4,)),
        ],
        compiler_params=small,
        name="rim",
    )(wet_mask, seams, fields)
    north = shifted(bottom, "row", 1)
    south = shifted(top, "row", -1)
    counts = lax.all_to_all(count, "col", split_axis=0, concat_axis=0, tiled=True)
    pack = jax.ShapeDtypeStruct((2 * (height + 8) + 16, ch), BF16)
    left, right = pl.pallas_call(
        side_kernel,
        out_shape=(pack, pack),
        in_specs=[SCALARS] + [WHOLE] * 4,
        out_specs=(WHOLE,) * 2,
        scratch_shapes=[pltpu.VMEM(pack.shape, F32)],
        compiler_params=small,
        name="side",
    )(wet_mask, north, south, lcols, rcols)
    left, right, counts = lax.optimization_barrier((left, right, counts))
    west = shifted(right, "col", 1)
    east = shifted(left, "col", -1)

    tile_shape = (tile, tile, ch)
    lines = 8 + (tile + 2) * tr_dev
    lines += -lines % 8
    keep, give = pl.pallas_call(
        conv_kernel,
        out_shape=(
            jax.ShapeDtypeStruct((chips,) + tile_shape, BF16),
            jax.ShapeDtypeStruct((half,) + tile_shape, BF16),
        ),
        in_specs=[SCALARS, SCALARS, WHOLE, IN_HBM] + [WHOLE] * 11,
        out_specs=(IN_PLACE, IN_PLACE),
        scratch_shapes=[
            pltpu.VMEM(fields.shape, BF16),
            pltpu.VMEM(fields.shape, BF16),
            pltpu.VMEM((height + 2, width, ch), BF16),
            pltpu.VMEM((height + 2, width, ch), BF16),
            pltpu.VMEM((height // 2, width, 2 * ch), BF16),
            pltpu.VMEM((4 * ch, 6 * ch), BF16),
            pltpu.VMEM((4 * ch, 6 * ch), BF16),
            pltpu.VMEM((2 * ch, 2 * ch), BF16),
            pltpu.VMEM((tr_dev, width, ch), F32),
            pltpu.VMEM((2,) + west.shape, F32),
            pltpu.VMEM((2, height + 8, ch), F32),
            pltpu.VMEM((2, height + 8, ch), F32),
            pltpu.VMEM((4, lines, ch), F32),
            pltpu.VMEM((lines, ch), F32),
            pltpu.VMEM((lines, ch), F32),
            pltpu.VMEM((lines, ch), F32),
            pltpu.VMEM((lines, ch), F32),
            pltpu.SemaphoreType.DMA((tr_dev,)),
            pltpu.SemaphoreType.DMA((face,)),
        ],
        compiler_params=params,
        name="both_convs",
    )(
        wet_mask, seams, counts, fields, north, south, west, east, lcols, rcols,
        kernel_one, bias_one[None], kernel_two, bias_two[None], mixing,
    )

    taken = lax.ppermute(give, "col", [(i, i ^ 1) for i in range(columns)])
    sending = pl.pallas_call(
        scatter_kernel,
        out_shape=jax.ShapeDtypeStruct(keep.shape, BF16),
        in_specs=[WHOLE, WHOLE, IN_PLACE],
        out_specs=IN_PLACE,
        scratch_shapes=[pltpu.SemaphoreType.DMA((half,))],
        input_output_aliases={2: 0},
        compiler_params=small,
        name="merge_mate",
    )(counts, taken, keep)
    groups = [[2 * k + c for k in range(chips)] for c in range(2)]
    arrived = lax.all_to_all(
        sending, "col", split_axis=0, concat_axis=0, tiled=True, axis_index_groups=groups
    )
    return pl.pallas_call(
        functools.partial(gather_kernel, tc_dev * columns),
        out_shape=jax.ShapeDtypeStruct((wet_dev,) + tile_shape, BF16),
        in_specs=[SCALARS, WHOLE],
        out_specs=IN_HBM,
        scratch_shapes=[pltpu.SemaphoreType.DMA((wet_dev,))],
        compiler_params=small,
        name="slot_order",
    )(wet_list, arrived)


def solution(mesh):
    return jax.shard_map(
        on_device,
        mesh=mesh,
        in_specs=(
            P("row", "col", None, None, None),
            P("row", "col"),
            P("row", "col", None),
            P(("row", "col")),
            P(),
            P(),
            P(),
            P(),
            P(),
        ),
        out_specs=P(("row", "col"), None, None, None),
        check_vma=False,
    )
```
